32 devices in a mesh: rep: 2 (over y), samp: 1, var: 16 (over z, x, core).
Axes of the slice: x: 2, y: 2, z: 4, core: 2. Of those that a mesh axis runs over, the one named last changes fastest.
Arguments:
- genotypes: bfloat16 [8192, 16384], P('samp', 'var'), may hold values from 0 to 2, as said below
- means: float32 [16384], P('var'), may hold values from 0.1 to 1
- scales: float32 [16384], P('var'), may hold values from 0.3 to 1
- causal: int32 [64, 1000], P('rep'), parts along dimension 0, may hold values from 0 to 16383
- effects: float32 [64, 1000], P('rep'), parts along dimension 0, may hold values from -0.19 to 0.19
- heritability: float32 [64], P('rep'), parts along dimension 0, may hold values from 0.1 to 0.9
- noise: bfloat16 [64, 8192], P('rep', 'samp'), parts along dimension 0, may hold values from -6 to 6
Outputs:
- phenotypes: bfloat16 [64, 8192], P('rep', ('samp', 'var')), parts along dimension 0
- scores: float32 [64, 16384], P('rep', ('var', 'samp')), parts along dimension 0
The draws below stay inside these ranges and needn't reach their ends.
There are 2 independent parts, one for each index of `rep`. The reference program is written for one: setup_inputs(seed, part) draws one part's arguments, and reference() takes and returns one part's arrays. A program takes and returns all parts, laid end to end along the dimension named above; an argument that names none is the same for every part. Nothing has to cross between parts.
Inputs may be any that keep to these rules, and one draw needn't show every extreme that they name: `genotypes`: dosages are 0, 1 or 2. `causal`: an index may repeat within a phenotype; its effects then add.
All inputs are finite; a program needn't handle non-finite values.
Results may differ from the reference program's by a relative error of at most 0.017.
Values may be sent and summed in bfloat16 or wider, within the bound.
No kernel may reach another device: no remote copies, remote signals or barrier semaphores. Data moves between devices by JAX's collectives and lax.ppermute only.
A program may use at most 64 MiB of HBM per device.

```python
import math
import jax
import jax.numpy as jnp
from jax import lax

PHENO = 32
CAUSAL = 1000
SAMPLES = 8192
VARIANTS = 16384


def draw_genotypes(key, part):
    freq_key = jax.random.fold_in(key, 11)
    first_key = jax.random.fold_in(key, 12)
    second_key = jax.random.fold_in(key, 13)
    freq = jax.random.uniform(freq_key, (1, VARIANTS), jnp.float32, 0.05, 0.5)
    first = (jax.random.uniform(first_key, (SAMPLES, VARIANTS), jnp.float32) < freq).astype(jnp.float32)
    second = (jax.random.uniform(second_key, (SAMPLES, VARIANTS), jnp.float32) < freq).astype(jnp.float32)
    return (first + second).astype(jnp.bfloat16)


def plant(result, stream_key, least, high):
    extent = result.shape
    place = [jax.random.randint(jax.random.fold_in(stream_key, axis), (), 0, extent[axis]) for axis in range(len(extent))]
    result = result.at[tuple(place)].set(least)
    longest = extent.index(max(extent))
    place[longest] = (place[longest] + 1) % extent[longest]
    return result.at[tuple(place)].set(high)


def block_levels(own_key, shape, cuts, least, top_value):
    loudness, own = 1.0, jax.random.fold_in(own_key, 6)
    for position, parts in cuts:
        heights = jnp.exp(jax.random.uniform(jax.random.fold_in(own, position), (parts,), jnp.float32, least / len(cuts), top_value / len(cuts)))
        loudness = loudness * jnp.repeat(heights, shape[position] // parts).reshape([-1 if axis == position else 1 for axis in range(len(shape))])
    return loudness


def normal_values(own_key, extent, width, reach, held_as=jnp.bfloat16):
    array = width * jax.random.normal(own_key, extent, jnp.float32)
    return jnp.clip(array, min=-reach, max=reach).astype(held_as)


def setup_inputs(seed: int = 0, part: int = 0) -> dict:
    key_of = jax.random.split(jax.random.key(seed), 8)
    part_keys = jax.random.split(jax.random.fold_in(key_of[7], part), 8)
    genotypes = draw_genotypes(jax.random.fold_in(key_of[7], 71), part)
    means = jnp.clip(0.1 + 0.9 * jax.random.uniform(key_of[1], (VARIANTS,), jnp.float32) ** block_levels(key_of[1], (VARIANTS,), ((0, 16),), -0.2, 0.2), 0.1, 1.0)
    scales = jnp.clip(jnp.exp(math.log(1.0) - 1.2039728 * jax.random.uniform(key_of[2], (VARIANTS,), jnp.float32) ** block_levels(key_of[2], (VARIANTS,), ((0, 16),), -0.2, 0.2)), 0.3, 1.0)
    causal = plant(jax.random.randint(part_keys[3], (PHENO, CAUSAL), 0, VARIANTS), jax.random.fold_in(part_keys[3], 1), 0, VARIANTS - 1).astype(jnp.int32)
    effects = normal_values(part_keys[4], (PHENO, CAUSAL), 0.0316, 0.19, jnp.float32)
    heritability = jnp.clip(jax.random.uniform(part_keys[5], (PHENO,), jnp.float32, 0.1, 0.9), 0.1, 0.9)
    noise = normal_values(part_keys[6], (PHENO, SAMPLES), 1.0, 6.0)
    return dict(genotypes=genotypes, means=means, scales=scales, causal=causal, effects=effects, heritability=heritability, noise=noise)


def reference(genotypes, means, scales, causal, effects, heritability, noise):
    pheno_rows = jnp.broadcast_to(jnp.arange(PHENO, dtype=jnp.int32)[:, None], causal.shape)
    beta = jnp.zeros((PHENO, VARIANTS), jnp.float32).at[pheno_rows, causal].add(effects.astype(jnp.float32))
    weights = (beta / scales[None, :]).astype(jnp.bfloat16)
    offset = lax.optimization_barrier(jnp.sum(weights.astype(jnp.float32) * means[None, :], axis=1))
    genetic = lax.dot_general(weights, genotypes, (((1,), (1,)), ((), ())), preferred_element_type=jnp.float32) - offset[:, None]
    heavy = jnp.sqrt(heritability)[:, None]
    light = jnp.sqrt(1.0 - heritability)[:, None]
    phenotypes = (heavy * genetic + light * noise.astype(jnp.float32)).astype(jnp.bfloat16)
    raw = jnp.dot(phenotypes, genotypes, preferred_element_type=jnp.float32)
    column_sum = lax.optimization_barrier(jnp.sum(phenotypes.astype(jnp.float32), axis=1))
    scores = (raw - column_sum[:, None] * means[None, :]) / (scales[None, :] * jnp.sqrt(jnp.float32(SAMPLES)))
    return (phenotypes, scores)
```

```python
import jax
import jax.numpy as jnp
from jax import lax
from jax.experimental import pallas as pl
from jax.experimental.pallas import tpu as pltpu
from jax.sharding import PartitionSpec as P

LANES = 128
MIB = 1 << 20


def evolve_kernel(
    blocks,
    share,
    order,
    genotypes_hbm,
    noise_hbm,
    means_hbm,
    scales_hbm,
    causal_hbm,
    effects_hbm,
    heritability_hbm,
    held_ref,
    send_ref,
    keep_ref,
    tail_ref,
    causal_ref,
    effects_ref,
    means_ref,
    scales_ref,
    heritability_ref,
    high_ref,
    low_ref,
    value_ref,
    beta_ref,
    weight_ref,
    noise_ref,
    block_sem,
    noise_sem,
    small_sem,
):
    pheno, variants = weight_ref.shape
    me = lax.axis_index("var")
    tails = tail_ref.shape[0]

    def fetch(r):
        start = pl.multiple_of((me ^ r) * share, share)
        return pltpu.make_async_copy(
            genotypes_hbm.at[pl.ds(start, share), :], held_ref.at[r], block_sem.at[r]
        )

    def fetch_noise(t):
        start = pl.multiple_of((me ^ (t * (blocks // tails))) * share, share)
        return pltpu.make_async_copy(
            noise_hbm.at[:, pl.ds(start, share)], noise_ref.at[t], noise_sem.at[t]
        )

    small = [
        pltpu.make_async_copy(source, target, small_sem.at[i])
        for i, (source, target) in enumerate(
            (
                (causal_hbm, causal_ref),
                (effects_hbm, effects_ref),
                (scales_hbm, scales_ref),
                (means_hbm, means_ref),
                (heritability_hbm, heritability_ref),
            )
        )
    ]
    for copy in small:
        copy.start()
    for t in range(tails):
        fetch_noise(t).start()
    for r in order:
        fetch(r).start()

    causal_count = causal_ref.shape[1]
    high_count = variants // LANES
    high_ref[...] = jnp.full(high_ref.shape, -1, jnp.int32)
    low_ref[...] = jnp.zeros(low_ref.shape, jnp.int32)
    value_ref[...] = jnp.zeros(value_ref.shape, jnp.float32)
    for copy in small:
        copy.wait()
    local = causal_ref[...] - me * variants
    inside = (local >= 0) & (local < variants)
    high_ref[:, :causal_count] = jnp.where(inside, local // LANES, -1)
    low_ref[:, :causal_count] = jnp.where(inside, local % LANES, 0)
    value_ref[:, :causal_count] = effects_ref[...]
    width = high_ref.shape[1]
    high_iota = lax.broadcasted_iota(jnp.int32, (high_count, width), 0)
    low_iota = lax.broadcasted_iota(jnp.int32, (LANES, width), 0)

    def build(p, carry):
        row = pl.ds(p, 1)
        value = jnp.where(high_ref[row, :] == high_iota, value_ref[row, :], 0.0)
        first = value.astype(jnp.bfloat16)
        rest = value - first.astype(jnp.float32)
        second = rest.astype(jnp.bfloat16)
        third = (rest - second.astype(jnp.float32)).astype(jnp.bfloat16)
        hits = jnp.where(low_ref[row, :] == low_iota, 1.0, 0.0).astype(jnp.bfloat16)
        parts = jnp.concatenate([first, second, third], axis=0)
        sums = lax.dot_general(
            parts, hits, (((1,), (1,)), ((), ())), preferred_element_type=jnp.float32
        )
        beta_ref[p] = (
            sums[:high_count] + sums[high_count : 2 * high_count] + sums[2 * high_count :]
        )
        return carry

    lax.fori_loop(0, pheno, build, 0, unroll=2)

    offset = jnp.zeros((pheno, LANES), jnp.float32)
    for h in range(high_count):
        lanes = slice(h * LANES, (h + 1) * LANES)
        weight = (beta_ref[:, h, :] / scales_ref[:, lanes]).astype(jnp.bfloat16)
        weight_ref[:, lanes] = weight
        offset += weight.astype(jnp.float32) * means_ref[:, lanes]
    offset = jnp.sum(offset, axis=1, keepdims=True)

    square = (pheno, pheno)
    diagonal = lax.broadcasted_iota(jnp.int32, square, 0) == lax.broadcasted_iota(
        jnp.int32, square, 1
    )
    share_genetic = jnp.sum(
        jnp.where(diagonal, jnp.broadcast_to(heritability_ref[...], square), 0.0),
        axis=1,
        keepdims=True,
    )
    heavy = jnp.sqrt(share_genetic)
    light = jnp.sqrt(1.0 - share_genetic)
    for t in range(tails):
        fetch_noise(t).wait()
        tail_ref[t] = light * noise_ref[t].astype(jnp.float32)

    weights = weight_ref[...]
    half = blocks // 2
    for i, r in enumerate(order):
        fetch(r).wait()
        part = heavy * (
            lax.dot_general(
                weights,
                held_ref[r],
                (((1,), (1,)), ((), ())),
                preferred_element_type=jnp.float32,
            )
            - offset
        )
        if i < half:
            send_ref[i] = part.astype(send_ref.dtype)
        else:
            keep_ref[i - half] = part.astype(keep_ref.dtype)


def scan_kernel(order, scale_back, *refs):
    held_ref, means_ref, scales_ref = refs[:3]
    pieces = refs[3:-1]
    out_ref = refs[-1]
    total = None
    column = None
    position = 0
    for piece in pieces:
        for j in range(piece.shape[0]):
            values = piece[j]
            part = jnp.dot(values, held_ref[order[position]], preferred_element_type=jnp.float32)
            sums = jnp.sum(values.astype(jnp.float32), axis=1, keepdims=True)
            total = part if total is None else total + part
            column = sums if column is None else column + sums
            position += 1
    if scale_back is None:
        out_ref[...] = total
    else:
        out_ref[...] = (total - column * means_ref[...]) / (scales_ref[...] * scale_back)


def on_device(genotypes, means, scales, causal, effects, heritability, noise):
    samples, variants = genotypes.shape
    pheno, causal_count = causal.shape
    blocks = lax.axis_size("var")
    samp = lax.axis_size("samp")
    share = samples // blocks
    bits = blocks.bit_length() - 1
    if blocks != 1 << bits or bits < 3:
        raise ValueError("var size")
    tails = blocks // 8

    def relative(core, group, tail):
        return core + 2 * group + 8 * tail

    order = [relative(c, g, t) for c in (1, 0) for g in (1, 2, 3, 0) for t in range(tails)]

    def pairs(k):
        return [(i, i ^ k) for i in range(blocks)]

    vmem = pl.BlockSpec(memory_space=pltpu.VMEM)
    hbm = pl.BlockSpec(memory_space=pltpu.HBM)
    means_row = means[None, :]
    scales_row = scales[None, :]
    width = -(-causal_count // LANES) * LANES
    half = blocks // 2

    held, send, keep, tail = pl.pallas_call(
        lambda *refs: evolve_kernel(blocks, share, order, *refs),
        out_shape=(
            jax.ShapeDtypeStruct((blocks, share, variants), genotypes.dtype),
            jax.ShapeDtypeStruct((half, pheno, share), jnp.bfloat16),
            jax.ShapeDtypeStruct((half, pheno, share), jnp.float32),
            jax.ShapeDtypeStruct((tails, pheno, share), jnp.float32),
        ),
        in_specs=[hbm] * 7,
        out_specs=[vmem] * 4,
        scratch_shapes=[
            pltpu.VMEM((pheno, causal_count), jnp.int32),
            pltpu.VMEM((pheno, causal_count), jnp.float32),
            pltpu.VMEM((1, variants), jnp.float32),
            pltpu.VMEM((1, variants), jnp.float32),
            pltpu.VMEM((1, pheno), jnp.float32),
            pltpu.VMEM((pheno, width), jnp.int32),
            pltpu.VMEM((pheno, width), jnp.int32),
            pltpu.VMEM((pheno, width), jnp.float32),
            pltpu.VMEM((pheno, variants // LANES, LANES), jnp.float32),
            pltpu.VMEM((pheno, variants), jnp.bfloat16),
            pltpu.VMEM((tails, pheno, share), jnp.bfloat16),
            pltpu.SemaphoreType.DMA((blocks,)),
            pltpu.SemaphoreType.DMA((tails,)),
            pltpu.SemaphoreType.DMA((5,)),
        ],
        compiler_params=pltpu.CompilerParams(vmem_limit_bytes=8 * MIB),
        name="evolve",
    )(
        *(
            pltpu.with_memory_space_constraint(x, pltpu.HBM)
            for x in (
                genotypes,
                noise,
                means_row,
                scales_row,
                causal,
                effects,
                heritability[None, :],
            )
        )
    )

    got = lax.ppermute(send, "var", pairs(1))
    chip = [
        keep[i * tails : (i + 1) * tails] + got[i * tails : (i + 1) * tails].astype(jnp.float32)
        for i in range(4)
    ]
    arrived = [
        lax.ppermute(chip[g - 1].astype(jnp.bfloat16), "var", pairs(2 * g)) for g in (1, 2, 3)
    ]
    total = chip[3]
    for other in arrived:
        total = total + other.astype(jnp.float32)

    step = 1
    while step < tails:
        mine = total.astype(jnp.bfloat16)
        other = lax.ppermute(mine, "var", pairs(8 * step))
        other = jnp.concatenate([other[t ^ step][None] for t in range(tails)], axis=0)
        total = mine.astype(jnp.float32) + other.astype(jnp.float32)
        step *= 2

    own = (total + tail).astype(jnp.bfloat16)
    phen_out = own[0]

    groups = {0: own}
    for g in (1, 2, 3):
        groups[g] = lax.ppermute(own, "var", pairs(2 * g))
    others = {g: lax.ppermute(groups[g], "var", pairs(1)) for g in range(4)}
    pieces = [groups[g] for g in range(4)] + [others[g] for g in range(4)]
    used = [relative(c, g, t) for c in (0, 1) for g in range(4) for t in range(tails)]

    alone = samp == 1
    total_samples = jnp.float32(samples * samp)
    scale_back = float(samples * samp) ** 0.5 if alone else None
    scores = pl.pallas_call(
        lambda *refs: scan_kernel(used, scale_back, *refs),
        out_shape=jax.ShapeDtypeStruct((pheno, variants), jnp.float32),
        in_specs=[vmem] * (3 + len(pieces)),
        out_specs=vmem,
        compiler_params=pltpu.CompilerParams(vmem_limit_bytes=8 * MIB),
        name="scan",
    )(held, means_row, scales_row, *pieces)
    if alone:
        return phen_out, scores

    column = sum(jnp.sum(piece.astype(jnp.float32), axis=(0, 2)) for piece in pieces)
    score_width = variants // samp
    score_start = lax.axis_index("samp") * score_width
    means_part = lax.dynamic_slice_in_dim(means, score_start, score_width, 0)
    scales_part = lax.dynamic_slice_in_dim(scales, score_start, score_width, 0)
    column_sum = lax.psum(column, "samp")
    correction = column_sum[:, None] * means_part[None, :]
    summed = lax.psum_scatter(scores, "samp", scatter_dimension=1, tiled=True)
    scores = (summed - correction) / (scales_part[None, :] * jnp.sqrt(total_samples))
    return phen_out, scores


def solution(mesh):
    in_specs = (
        P("samp", "var"),
        P("var"),
        P("var"),
        P("rep", None),
        P("rep", None),
        P("rep"),
        P("rep", "samp"),
    )
    out_specs = (P("rep", ("samp", "var")), P("rep", ("var", "samp")))
    return jax.shard_map(
        on_device, mesh=mesh, in_specs=in_specs, out_specs=out_specs, check_vma=False
    )
```

```python
import jax
import jax.numpy as jnp
from jax import lax
from jax.experimental import pallas as pl
from jax.experimental.pallas import tpu as pltpu
from jax.sharding import PartitionSpec as P

LANES = 128
MIB = 1 << 20
SMALL = jnp.float8_e4m3fn
LARGEST = 448.0
SHIFT = 16.0
EFFECT_SCALE = 1024.0


def row_scale(values):
    largest = jnp.max(jnp.abs(values), axis=1, keepdims=True)
    scale = jnp.full_like(largest, 2.0**-30)
    for step in (32, 16, 8, 4, 2, 1):
        raised = scale * 2.0**step
        scale = jnp.where(largest * raised <= LARGEST, raised, scale)
    return scale


def split(values, count):
    parts = []
    for i in range(count):
        part = values.astype(SMALL)
        parts.append(part)
        if i + 1 < count:
            values = (values - part.astype(jnp.float32)) * SHIFT
    return jnp.concatenate(parts, axis=0)


def join(sums, count):
    rows = sums.shape[0] // count
    total = sums[(count - 1) * rows :]
    for i in reversed(range(count - 1)):
        total = sums[i * rows : (i + 1) * rows] + total * (1.0 / SHIFT)
    return total


def evolve_kernel(
    blocks,
    share,
    flight,
    relative_of,
    genotypes_hbm,
    noise_hbm,
    means_hbm,
    scales_hbm,
    causal_hbm,
    effects_hbm,
    heritability_hbm,
    held_ref,
    send_ref,
    keep_ref,
    tail_ref,
    staged_ref,
    causal_ref,
    effects_ref,
    means_ref,
    scales_ref,
    heritability_ref,
    high_ref,
    low_ref,
    value_ref,
    beta_ref,
    weight_ref,
    noise_ref,
    block_sem,
    noise_sem,
    small_sem,
):
    pheno, variants = weight_ref.shape
    me = lax.axis_index("var")
    tails = tail_ref.shape[0]
    half = blocks // 2

    def fetch(i):
        start = pl.multiple_of((me ^ relative_of(i)) * share, share)
        return pltpu.make_async_copy(
            genotypes_hbm.at[pl.ds(start, share), :], staged_ref.at[i], block_sem.at[i]
        )

    def fetch_noise(t):
        start = pl.multiple_of((me ^ (t * (blocks // tails))) * share, share)
        return pltpu.make_async_copy(
            noise_hbm.at[:, pl.ds(start, share)], noise_ref.at[t], noise_sem.at[t]
        )

    small = [
        pltpu.make_async_copy(source, target, small_sem.at[i])
        for i, (source, target) in enumerate(
            (
                (causal_hbm, causal_ref),
                (effects_hbm, effects_ref),
                (scales_hbm, scales_ref),
                (means_hbm, means_ref),
                (heritability_hbm, heritability_ref),
            )
        )
    ]
    for copy in small:
        copy.start()
    for i in range(flight):
        fetch(i).start()
    for t in range(tails):
        fetch_noise(t).start()

    causal_count = causal_ref.shape[1]
    high_count = variants // LANES
    high_ref[...] = jnp.full(high_ref.shape, -1, jnp.int32)
    low_ref[...] = jnp.zeros(low_ref.shape, jnp.int32)
    value_ref[...] = jnp.zeros(value_ref.shape, jnp.float32)
    for copy in small:
        copy.wait()
    local = causal_ref[...] - me * variants
    inside = (local >= 0) & (local < variants)
    high_ref[:, :causal_count] = jnp.where(inside, local // LANES, -1)
    low_ref[:, :causal_count] = jnp.where(inside, local % LANES, 0)
    value_ref[:, :causal_count] = effects_ref[...] * EFFECT_SCALE
    width = high_ref.shape[1]
    high_iota = lax.broadcasted_iota(jnp.int32, (high_count, width), 0)
    low_iota = lax.broadcasted_iota(jnp.int32, (LANES, width), 0).astype(jnp.int16)

    def build(p):
        row = pl.ds(p, 1)
        value = jnp.where(high_ref[row, :] == high_iota, value_ref[row, :], 0.0)
        low = jnp.broadcast_to(low_ref[row, :], (LANES, width)).astype(jnp.int16)
        hits = jnp.where(low == low_iota, jnp.bfloat16(1), jnp.bfloat16(0)).astype(SMALL)
        sums = lax.dot_general(
            split(value, 4), hits, (((1,), (1,)), ((), ())), preferred_element_type=jnp.float32
        )
        beta_ref[p] = join(sums, 4) * (1.0 / EFFECT_SCALE)

    per_step = -(-pheno // half)

    def first(i, carry):
        fetch(i).wait()

        @pl.when(i + flight < blocks)
        def _():
            fetch(i + flight).start()

        held_ref[i] = staged_ref[i].astype(SMALL)
        for j in range(per_step):
            build(jnp.minimum(i * per_step + j, pheno - 1))
        return carry

    lax.fori_loop(0, half, first, 0)

    offset = jnp.zeros((pheno, LANES), jnp.float32)
    for h in range(high_count):
        lanes = slice(h * LANES, (h + 1) * LANES)
        weight = (beta_ref[:, h, :] / scales_ref[:, lanes]).astype(jnp.bfloat16)
        weight = weight.astype(jnp.float32)
        weight_ref[:, lanes] = weight
        offset += weight * means_ref[:, lanes]
    offset = jnp.sum(offset, axis=1, keepdims=True)

    square = (pheno, pheno)
    diagonal = lax.broadcasted_iota(jnp.int32, square, 0) == lax.broadcasted_iota(
        jnp.int32, square, 1
    )
    share_genetic = jnp.sum(
        jnp.where(diagonal, jnp.broadcast_to(heritability_ref[...], square), 0.0),
        axis=1,
        keepdims=True,
    )
    heavy = jnp.sqrt(share_genetic)
    light = jnp.sqrt(1.0 - share_genetic)
    for t in range(tails):
        fetch_noise(t).wait()
        tail_ref[t] = light * noise_ref[t].astype(jnp.float32)

    scale = row_scale(weight_ref[...])
    weights = split(weight_ref[...] * scale, 2)
    factor = heavy / scale
    shift = heavy * offset

    def partial(i):
        sums = lax.dot_general(
            weights, held_ref[i], (((1,), (1,)), ((), ())), preferred_element_type=jnp.float32
        )
        return join(sums, 2) * factor - shift

    def second(i, carry):
        send_ref[i] = partial(i).astype(send_ref.dtype)
        late = half + i
        fetch(late).wait()

        @pl.when(late + flight < blocks)
        def _():
            fetch(late + flight).start()

        held_ref[late] = staged_ref[late].astype(SMALL)
        keep_ref[i] = partial(late).astype(keep_ref.dtype)
        return carry

    lax.fori_loop(0, half, second, 0)


def scan_kernel(order, scale_back, *refs):
    held_ref, means_ref, scales_ref = refs[:3]
    pieces = refs[3:-2]
    phen_ref, out_ref = refs[-2:]
    values = [piece[j].astype(jnp.float32) for piece in pieces for j in range(piece.shape[0])]
    phen_ref[...] = pieces[0][0]
    largest = values[0]
    column = values[0]
    for value in values[1:]:
        largest = jnp.maximum(jnp.abs(largest), jnp.abs(value))
        column = column + value
    column = jnp.sum(column, axis=1, keepdims=True)
    scale = row_scale(largest)
    total = None
    for i, value in enumerate(values):
        part = jnp.dot(
            split(value * scale, 2), held_ref[order[i]], preferred_element_type=jnp.float32
        )
        total = part if total is None else total + part
    total = join(total, 2) / scale
    if scale_back is None:
        out_ref[...] = total
    else:
        out_ref[...] = (total - column * means_ref[...]) / (scales_ref[...] * scale_back)


def on_device(genotypes, means, scales, causal, effects, heritability, noise):
    samples, variants = genotypes.shape
    pheno, causal_count = causal.shape
    blocks = lax.axis_size("var")
    samp = lax.axis_size("samp")
    share = samples // blocks
    bits = blocks.bit_length() - 1
    if blocks != 1 << bits or bits < 3:
        raise ValueError("var size")
    tails = blocks // 8

    half = blocks // 2

    def relative_of(i):
        core = 1 - i // half
        group = (i % half // tails + 1) % 4
        return core + 2 * group + 8 * (i % tails)

    def position(core, group, tail):
        return (1 - core) * half + (group + 3) % 4 * tails + tail

    def pairs(k):
        return [(i, i ^ k) for i in range(blocks)]

    vmem = pl.BlockSpec(memory_space=pltpu.VMEM)
    hbm = pl.BlockSpec(memory_space=pltpu.HBM)
    means_row = means[None, :]
    scales_row = scales[None, :]
    width = -(-causal_count // LANES) * LANES

    held, send, keep, tail = pl.pallas_call(
        lambda *refs: evolve_kernel(blocks, share, half, relative_of, *refs),
        out_shape=(
            jax.ShapeDtypeStruct((blocks, share, variants), SMALL),
            jax.ShapeDtypeStruct((half, pheno, share), jnp.bfloat16),
            jax.ShapeDtypeStruct((half, pheno, share), jnp.float32),
            jax.ShapeDtypeStruct((tails, pheno, share), jnp.float32),
        ),
        in_specs=[hbm] * 7,
        out_specs=[vmem] * 4,
        scratch_shapes=[
            pltpu.VMEM((blocks, share, variants), genotypes.dtype),
            pltpu.VMEM((pheno, causal_count), jnp.int32),
            pltpu.VMEM((pheno, causal_count), jnp.float32),
            pltpu.VMEM((1, variants), jnp.float32),
            pltpu.VMEM((1, variants), jnp.float32),
            pltpu.VMEM((1, pheno), jnp.float32),
            pltpu.VMEM((pheno, width), jnp.int32),
            pltpu.VMEM((pheno, width), jnp.int32),
            pltpu.VMEM((pheno, width), jnp.float32),
            pltpu.VMEM((pheno, variants // LANES, LANES), jnp.float32),
            pltpu.VMEM((pheno, variants), jnp.float32),
            pltpu.VMEM((tails, pheno, share), jnp.bfloat16),
            pltpu.SemaphoreType.DMA((blocks,)),
            pltpu.SemaphoreType.DMA((tails,)),
            pltpu.SemaphoreType.DMA((5,)),
        ],
        compiler_params=pltpu.CompilerParams(vmem_limit_bytes=24 * MIB),
        name="evolve",
    )(
        *(
            pltpu.with_memory_space_constraint(x, pltpu.HBM)
            for x in (
                genotypes,
                noise,
                means_row,
                scales_row,
                causal,
                effects,
                heritability[None, :],
            )
        )
    )

    got = lax.ppermute(send, "var", pairs(1))
    chip = [
        keep[i * tails : (i + 1) * tails] + got[i * tails : (i + 1) * tails].astype(jnp.float32)
        for i in range(4)
    ]
    arrived = [
        lax.ppermute(chip[g - 1].astype(jnp.bfloat16), "var", pairs(2 * g)) for g in (1, 2, 3)
    ]
    total = chip[3]
    for other in arrived:
        total = total + other.astype(jnp.float32)

    step = 1
    while step < tails:
        mine = total.astype(jnp.bfloat16)
        other = lax.ppermute(mine, "var", pairs(8 * step))
        other = jnp.concatenate([other[t ^ step][None] for t in range(tails)], axis=0)
        total = mine.astype(jnp.float32) + other.astype(jnp.float32)
        step *= 2

    own = (total + tail).astype(jnp.bfloat16)
    groups = {0: own}
    for g in (1, 2, 3):
        groups[g] = lax.ppermute(own, "var", pairs(2 * g))
    others = {g: lax.ppermute(groups[g], "var", pairs(1)) for g in range(4)}
    pieces = [groups[g] for g in range(4)] + [others[g] for g in range(4)]
    used = [position(c, g, t) for c in (0, 1) for g in range(4) for t in range(tails)]

    alone = samp == 1
    total_samples = jnp.float32(samples * samp)
    scale_back = float(samples * samp) ** 0.5 if alone else None
    phen_out, scores = pl.pallas_call(
        lambda *refs: scan_kernel(used, scale_back, *refs),
        out_shape=(
            jax.ShapeDtypeStruct((pheno, share), jnp.bfloat16),
            jax.ShapeDtypeStruct((pheno, variants), jnp.float32),
        ),
        in_specs=[vmem] * (3 + len(pieces)),
        out_specs=[vmem] * 2,
        compiler_params=pltpu.CompilerParams(vmem_limit_bytes=8 * MIB),
        name="scan",
    )(held, means_row, scales_row, *pieces)
    if alone:
        return phen_out, scores

    column = sum(jnp.sum(piece.astype(jnp.float32), axis=(0, 2)) for piece in pieces)
    score_width = variants // samp
    score_start = lax.axis_index("samp") * score_width
    means_part = lax.dynamic_slice_in_dim(means, score_start, score_width, 0)
    scales_part = lax.dynamic_slice_in_dim(scales, score_start, score_width, 0)
    column_sum = lax.psum(column, "samp")
    correction = column_sum[:, None] * means_part[None, :]
    summed = lax.psum_scatter(scores, "samp", scatter_dimension=1, tiled=True)
    scores = (summed - correction) / (scales_part[None, :] * jnp.sqrt(total_samples))
    return phen_out, scores


def solution(mesh):
    in_specs = (
        P("samp", "var"),
        P("var"),
        P("var"),
        P("rep", None),
        P("rep", None),
        P("rep"),
        P("rep", "samp"),
    )
    out_specs = (P("rep", ("samp", "var")), P("rep", ("var", "samp")))
    return jax.shard_map(
        on_device, mesh=mesh, in_specs=in_specs, out_specs=out_specs, check_vma=False
    )
```

```python
import jax
import jax.numpy as jnp
from jax import lax
from jax.experimental import pallas as pl
from jax.experimental.pallas import tpu as pltpu
from jax.sharding import PartitionSpec as P

LANES = 128
MIB = 1 << 20
SMALL = jnp.float8_e4m3fn
LARGEST = 448.0
FLIGHT = 3
SHIFT = 16.0
EFFECT_SCALE = 1024.0


def row_scale(values):
    largest = jnp.max(jnp.abs(values), axis=1, keepdims=True)
    scale = jnp.full_like(largest, 2.0**-30)
    for step in (32, 16, 8, 4, 2, 1):
        raised = scale * 2.0**step
        scale = jnp.where(largest * raised <= LARGEST, raised, scale)
    return scale


def split(values, count):
    parts = []
    for i in range(count):
        part = values.astype(SMALL)
        parts.append(part)
        if i + 1 < count:
            values = (values - part.astype(jnp.float32)) * SHIFT
    return jnp.concatenate(parts, axis=0)


def join(sums, count):
    rows = sums.shape[0] // count
    total = sums[(count - 1) * rows :]
    for i in reversed(range(count - 1)):
        total = sums[i * rows : (i + 1) * rows] + total * (1.0 / SHIFT)
    return total


def evolve_kernel(
    blocks,
    share,
    flight,
    relative_of,
    genotypes_hbm,
    noise_hbm,
    means_hbm,
    scales_hbm,
    causal_hbm,
    effects_hbm,
    heritability_hbm,
    held_ref,
    send_ref,
    keep_ref,
    tail_ref,
    staged_ref,
    causal_ref,
    effects_ref,
    means_ref,
    scales_ref,
    heritability_ref,
    high_ref,
    low_ref,
    value_ref,
    beta_ref,
    weight_ref,
    noise_ref,
    block_sem,
    noise_sem,
    small_sem,
):
    pheno, variants = weight_ref.shape
    me = lax.axis_index("var")
    tails = tail_ref.shape[0]
    half = blocks // 2

    def fetch(i):
        start = pl.multiple_of((me ^ relative_of(i)) * share, share)
        return pltpu.make_async_copy(
            genotypes_hbm.at[pl.ds(start, share), :], staged_ref.at[i], block_sem.at[i]
        )

    def fetch_noise(t):
        start = pl.multiple_of((me ^ (t * (blocks // tails))) * share, share)
        return pltpu.make_async_copy(
            noise_hbm.at[:, pl.ds(start, share)], noise_ref.at[t], noise_sem.at[t]
        )

    small = [
        pltpu.make_async_copy(source, target, small_sem.at[i])
        for i, (source, target) in enumerate(
            (
                (causal_hbm, causal_ref),
                (effects_hbm, effects_ref),
                (scales_hbm, scales_ref),
                (means_hbm, means_ref),
                (heritability_hbm, heritability_ref),
            )
        )
    ]
    for copy in small:
        copy.start()
    for t in range(tails):
        fetch_noise(t).start()

    causal_count = causal_ref.shape[1]
    high_count = variants // LANES
    high_ref[...] = jnp.full(high_ref.shape, -1, jnp.int32)
    low_ref[...] = jnp.zeros(low_ref.shape, jnp.int32)
    value_ref[...] = jnp.zeros(value_ref.shape, jnp.float32)
    for copy in small:
        copy.wait()
    for i in range(flight):
        fetch(i).start()
    local = causal_ref[...] - me * variants
    inside = (local >= 0) & (local < variants)
    high_ref[:, :causal_count] = jnp.where(inside, local // LANES, -1)
    low_ref[:, :causal_count] = jnp.where(inside, local % LANES, 0)
    value_ref[:, :causal_count] = effects_ref[...] * EFFECT_SCALE
    width = high_ref.shape[1]
    high_iota = lax.broadcasted_iota(jnp.int32, (high_count, width), 0)
    low_iota = lax.broadcasted_iota(jnp.int32, (LANES, width), 0).astype(jnp.int16)

    def build(p):
        row = pl.ds(p, 1)
        value = jnp.where(high_ref[row, :] == high_iota, value_ref[row, :], 0.0)
        low = jnp.broadcast_to(low_ref[row, :], (LANES, width)).astype(jnp.int16)
        hits = jnp.where(low == low_iota, jnp.bfloat16(1), jnp.bfloat16(0)).astype(SMALL)
        sums = lax.dot_general(
            split(value, 4), hits, (((1,), (1,)), ((), ())), preferred_element_type=jnp.float32
        )
        beta_ref[p] = join(sums, 4) * (1.0 / EFFECT_SCALE)

    steps = half
    per_step = -(-pheno // steps)

    def build_step(i, carry):
        @pl.when(flight + i < blocks)
        def _():
            fetch(flight + i).start()

        for j in range(per_step):
            build(jnp.minimum(i * per_step + j, pheno - 1))
        return carry

    lax.fori_loop(0, steps, build_step, 0, unroll=True)
    for i in range(flight + steps, blocks):
        fetch(i).start()

    offset = jnp.zeros((pheno, LANES), jnp.float32)
    for h in range(high_count):
        lanes = slice(h * LANES, (h + 1) * LANES)
        weight = (beta_ref[:, h, :] / scales_ref[:, lanes]).astype(jnp.bfloat16)
        weight = weight.astype(jnp.float32)
        weight_ref[:, lanes] = weight
        offset += weight * means_ref[:, lanes]
    offset = jnp.sum(offset, axis=1, keepdims=True)

    square = (pheno, pheno)
    diagonal = lax.broadcasted_iota(jnp.int32, square, 0) == lax.broadcasted_iota(
        jnp.int32, square, 1
    )
    share_genetic = jnp.sum(
        jnp.where(diagonal, jnp.broadcast_to(heritability_ref[...], square), 0.0),
        axis=1,
        keepdims=True,
    )
    heavy = jnp.sqrt(share_genetic)
    light = jnp.sqrt(1.0 - share_genetic)
    for t in range(tails):
        fetch_noise(t).wait()
        tail_ref[t] = light * noise_ref[t].astype(jnp.float32)

    scale = row_scale(weight_ref[...])
    weights = split(weight_ref[...] * scale, 2)
    factor = heavy / scale
    shift = heavy * offset

    def convert(i):
        fetch(i).wait()
        held_ref[i] = staged_ref[i].astype(SMALL)

    def partial(i):
        sums = lax.dot_general(
            weights, held_ref[i], (((1,), (1,)), ((), ())), preferred_element_type=jnp.float32
        )
        return join(sums, 2) * factor - shift

    convert(0)

    def multiply_send(i, carry):
        convert(i + 1)
        send_ref[i] = partial(i).astype(send_ref.dtype)
        return carry

    def multiply_keep(i, carry):
        convert(half + i + 1)
        keep_ref[i] = partial(half + i).astype(keep_ref.dtype)
        return carry

    lax.fori_loop(0, half, multiply_send, 0, unroll=True)
    lax.fori_loop(0, half - 1, multiply_keep, 0, unroll=True)
    keep_ref[half - 1] = partial(blocks - 1).astype(keep_ref.dtype)


def scan_kernel(order, scale_back, *refs):
    held_ref, means_ref, scales_ref = refs[:3]
    pieces = refs[3:-2]
    phen_ref, out_ref = refs[-2:]
    values = [piece[j].astype(jnp.float32) for piece in pieces for j in range(piece.shape[0])]
    phen_ref[...] = pieces[0][0]
    largest = values[0]
    column = values[0]
    for value in values[1:]:
        largest = jnp.maximum(jnp.abs(largest), jnp.abs(value))
        column = column + value
    column = jnp.sum(column, axis=1, keepdims=True)
    scale = row_scale(largest)
    total = None
    for i, value in enumerate(values):
        part = jnp.dot(
            split(value * scale, 2), held_ref[order[i]], preferred_element_type=jnp.float32
        )
        total = part if total is None else total + part
    total = join(total, 2) / scale
    if scale_back is None:
        out_ref[...] = total
    else:
        out_ref[...] = (total - column * means_ref[...]) / (scales_ref[...] * scale_back)


def on_device(genotypes, means, scales, causal, effects, heritability, noise):
    samples, variants = genotypes.shape
    pheno, causal_count = causal.shape
    blocks = lax.axis_size("var")
    samp = lax.axis_size("samp")
    share = samples // blocks
    bits = blocks.bit_length() - 1
    if blocks != 1 << bits or bits < 3:
        raise ValueError("var size")
    tails = blocks // 8

    half = blocks // 2

    def relative_of(i):
        core = 1 - i // half
        group = (i % half // tails + 1) % 4
        return core + 2 * group + 8 * (i % tails)

    def position(core, group, tail):
        return (1 - core) * half + (group + 3) % 4 * tails + tail

    def pairs(k):
        return [(i, i ^ k) for i in range(blocks)]

    vmem = pl.BlockSpec(memory_space=pltpu.VMEM)
    hbm = pl.BlockSpec(memory_space=pltpu.HBM)
    means_row = means[None, :]
    scales_row = scales[None, :]
    width = -(-causal_count // LANES) * LANES

    held, send, keep, tail = pl.pallas_call(
        lambda *refs: evolve_kernel(blocks, share, FLIGHT, relative_of, *refs),
        out_shape=(
            jax.ShapeDtypeStruct((blocks, share, variants), SMALL),
            jax.ShapeDtypeStruct((half, pheno, share), jnp.bfloat16),
            jax.ShapeDtypeStruct((half, pheno, share), jnp.float32),
            jax.ShapeDtypeStruct((tails, pheno, share), jnp.float32),
        ),
        in_specs=[hbm] * 7,
        out_specs=[vmem] * 4,
        scratch_shapes=[
            pltpu.VMEM((blocks, share, variants), genotypes.dtype),
            pltpu.VMEM((pheno, causal_count), jnp.int32),
            pltpu.VMEM((pheno, causal_count), jnp.float32),
            pltpu.VMEM((1, variants), jnp.float32),
            pltpu.VMEM((1, variants), jnp.float32),
            pltpu.VMEM((1, pheno), jnp.float32),
            pltpu.VMEM((pheno, width), jnp.int32),
            pltpu.VMEM((pheno, width), jnp.int32),
            pltpu.VMEM((pheno, width), jnp.float32),
            pltpu.VMEM((pheno, variants // LANES, LANES), jnp.float32),
            pltpu.VMEM((pheno, variants), jnp.float32),
            pltpu.VMEM((tails, pheno, share), jnp.bfloat16),
            pltpu.SemaphoreType.DMA((blocks,)),
            pltpu.SemaphoreType.DMA((tails,)),
            pltpu.SemaphoreType.DMA((5,)),
        ],
        compiler_params=pltpu.CompilerParams(vmem_limit_bytes=24 * MIB),
        name="evolve",
    )(
        *(
            pltpu.with_memory_space_constraint(x, pltpu.HBM)
            for x in (
                genotypes,
                noise,
                means_row,
                scales_row,
                causal,
                effects,
                heritability[None, :],
            )
        )
    )

    got = lax.ppermute(send, "var", pairs(1))
    chip = [
        keep[i * tails : (i + 1) * tails] + got[i * tails : (i + 1) * tails].astype(jnp.float32)
        for i in range(4)
    ]
    arrived = [
        lax.ppermute(chip[g - 1].astype(jnp.bfloat16), "var", pairs(2 * g)) for g in (1, 2, 3)
    ]
    total = chip[3]
    for other in arrived:
        total = total + other.astype(jnp.float32)

    step = 1
    while step < tails:
        mine = total.astype(jnp.bfloat16)
        other = lax.ppermute(mine, "var", pairs(8 * step))
        other = jnp.concatenate([other[t ^ step][None] for t in range(tails)], axis=0)
        total = mine.astype(jnp.float32) + other.astype(jnp.float32)
        step *= 2

    own = (total + tail).astype(jnp.bfloat16)
    groups = {0: own}
    for g in (1, 2, 3):
        groups[g] = lax.ppermute(own, "var", pairs(2 * g))
    others = {g: lax.ppermute(groups[g], "var", pairs(1)) for g in range(4)}
    pieces = [groups[g] for g in range(4)] + [others[g] for g in range(4)]
    used = [position(c, g, t) for c in (0, 1) for g in range(4) for t in range(tails)]

    alone = samp == 1
    total_samples = jnp.float32(samples * samp)
    scale_back = float(samples * samp) ** 0.5 if alone else None
    phen_out, scores = pl.pallas_call(
        lambda *refs: scan_kernel(used, scale_back, *refs),
        out_shape=(
            jax.ShapeDtypeStruct((pheno, share), jnp.bfloat16),
            jax.ShapeDtypeStruct((pheno, variants), jnp.float32),
        ),
        in_specs=[vmem] * (3 + len(pieces)),
        out_specs=[vmem] * 2,
        compiler_params=pltpu.CompilerParams(vmem_limit_bytes=8 * MIB),
        name="scan",
    )(held, means_row, scales_row, *pieces)
    if alone:
        return phen_out, scores

    column = sum(jnp.sum(piece.astype(jnp.float32), axis=(0, 2)) for piece in pieces)
    score_width = variants // samp
    score_start = lax.axis_index("samp") * score_width
    means_part = lax.dynamic_slice_in_dim(means, score_start, score_width, 0)
    scales_part = lax.dynamic_slice_in_dim(scales, score_start, score_width, 0)
    column_sum = lax.psum(column, "samp")
    correction = column_sum[:, None] * means_part[None, :]
    summed = lax.psum_scatter(scores, "samp", scatter_dimension=1, tiled=True)
    scores = (summed - correction) / (scales_part[None, :] * jnp.sqrt(total_samples))
    return phen_out, scores


def solution(mesh):
    in_specs = (
        P("samp", "var"),
        P("var"),
        P("var"),
        P("rep", None),
        P("rep", None),
        P("rep"),
        P("rep", "samp"),
    )
    out_specs = (P("rep", ("samp", "var")), P("rep", ("var", "samp")))
    return jax.shard_map(
        on_device, mesh=mesh, in_specs=in_specs, out_specs=out_specs, check_vma=False
    )
```

```python
import jax
import jax.numpy as jnp
from jax import lax
from jax.experimental import pallas as pl
from jax.experimental.pallas import tpu as pltpu
from jax.sharding import PartitionSpec as P

LANES = 128
MIB = 1 << 20
SMALL = jnp.float8_e4m3fn
LARGEST = 448.0
FLIGHT = 3
SHIFT = 16.0
EFFECT_SCALE = 1024.0


def row_scale(values):
    largest = jnp.max(jnp.abs(values), axis=1, keepdims=True)
    scale = jnp.full_like(largest, 2.0**-30)
    for step in (32, 16, 8, 4, 2, 1):
        raised = scale * 2.0**step
        scale = jnp.where(largest * raised <= LARGEST, raised, scale)
    return scale


def split(values, count):
    parts = []
    for i in range(count):
        part = values.astype(SMALL)
        parts.append(part)
        if i + 1 < count:
            values = (values - part.astype(jnp.float32)) * SHIFT
    return jnp.concatenate(parts, axis=0)


def join(sums, count):
    rows = sums.shape[0] // count
    total = sums[(count - 1) * rows :]
    for i in reversed(range(count - 1)):
        total = sums[i * rows : (i + 1) * rows] + total * (1.0 / SHIFT)
    return total


def evolve_kernel(
    blocks,
    share,
    flight,
    relative_of,
    genotypes_hbm,
    noise_hbm,
    means_hbm,
    scales_hbm,
    causal_hbm,
    effects_hbm,
    heritability_hbm,
    held_ref,
    send_ref,
    keep_ref,
    tail_ref,
    staged_ref,
    causal_ref,
    effects_ref,
    means_ref,
    scales_ref,
    heritability_ref,
    high_ref,
    low_ref,
    value_ref,
    beta_ref,
    weight_ref,
    noise_ref,
    block_sem,
    noise_sem,
    small_sem,
):
    pheno, variants = weight_ref.shape
    me = lax.axis_index("var")
    tails = tail_ref.shape[0]
    half = blocks // 2

    def fetch(i):
        start = pl.multiple_of((me ^ relative_of(i)) * share, share)
        return pltpu.make_async_copy(
            genotypes_hbm.at[pl.ds(start, share), :], staged_ref.at[i], block_sem.at[i]
        )

    def fetch_noise(t):
        start = pl.multiple_of((me ^ (t * (blocks // tails))) * share, share)
        return pltpu.make_async_copy(
            noise_hbm.at[:, pl.ds(start, share)], noise_ref.at[t], noise_sem.at[t]
        )

    small = [
        pltpu.make_async_copy(source, target, small_sem.at[i])
        for i, (source, target) in enumerate(
            (
                (causal_hbm, causal_ref),
                (effects_hbm, effects_ref),
                (scales_hbm, scales_ref),
                (means_hbm, means_ref),
                (heritability_hbm, heritability_ref),
            )
        )
    ]
    for copy in small:
        copy.start()
    for t in range(tails):
        fetch_noise(t).start()

    causal_count = causal_ref.shape[1]
    high_count = variants // LANES
    high_ref[...] = jnp.full(high_ref.shape, -1, jnp.int32)
    low_ref[...] = jnp.zeros(low_ref.shape, jnp.int32)
    value_ref[...] = jnp.zeros(value_ref.shape, jnp.float32)
    for copy in small[:2]:
        copy.wait()
    for i in range(flight):
        fetch(i).start()
    local = causal_ref[...] - me * variants
    inside = (local >= 0) & (local < variants)
    high_ref[:, :causal_count] = jnp.where(inside, local // LANES, -1)
    low_ref[:, :causal_count] = jnp.where(inside, local % LANES, 0)
    value_ref[:, :causal_count] = effects_ref[...] * EFFECT_SCALE
    width = high_ref.shape[1]
    high_iota = lax.broadcasted_iota(jnp.int32, (high_count, width), 0)
    low_iota = lax.broadcasted_iota(jnp.int32, (LANES, width), 0).astype(jnp.int16)

    def build(p):
        row = pl.ds(p, 1)
        value = jnp.where(high_ref[row, :] == high_iota, value_ref[row, :], 0.0)
        low = jnp.broadcast_to(low_ref[row, :], (LANES, width)).astype(jnp.int16)
        hits = jnp.where(low == low_iota, jnp.bfloat16(1), jnp.bfloat16(0)).astype(SMALL)
        sums = lax.dot_general(
            split(value, 4), hits, (((1,), (1,)), ((), ())), preferred_element_type=jnp.float32
        )
        beta_ref[p] = join(sums, 4) * (1.0 / EFFECT_SCALE)

    steps = half
    per_step = -(-pheno // steps)

    def build_step(i, carry):
        @pl.when(flight + i < blocks)
        def _():
            fetch(flight + i).start()

        for j in range(per_step):
            build(jnp.minimum(i * per_step + j, pheno - 1))
        return carry

    lax.fori_loop(0, steps, build_step, 0, unroll=True)
    for i in range(flight + steps, blocks):
        fetch(i).start()

    for copy in small[2:]:
        copy.wait()
    offset = jnp.zeros((pheno, LANES), jnp.float32)
    for h in range(high_count):
        lanes = slice(h * LANES, (h + 1) * LANES)
        weight = (beta_ref[:, h, :] / scales_ref[:, lanes]).astype(jnp.bfloat16)
        weight = weight.astype(jnp.float32)
        weight_ref[:, lanes] = weight
        offset += weight * means_ref[:, lanes]
    offset = jnp.sum(offset, axis=1, keepdims=True)

    square = (pheno, pheno)
    diagonal = lax.broadcasted_iota(jnp.int32, square, 0) == lax.broadcasted_iota(
        jnp.int32, square, 1
    )
    share_genetic = jnp.sum(
        jnp.where(diagonal, jnp.broadcast_to(heritability_ref[...], square), 0.0),
        axis=1,
        keepdims=True,
    )
    heavy = jnp.sqrt(share_genetic)
    light = jnp.sqrt(1.0 - share_genetic)
    scale = row_scale(weight_ref[...])
    weights = split(weight_ref[...] * scale, 2)
    factor = heavy / scale
    shift = heavy * offset

    def convert(i):
        fetch(i).wait()
        held_ref[i] = staged_ref[i].astype(SMALL)

    def partial(i):
        sums = lax.dot_general(
            weights, held_ref[i], (((1,), (1,)), ((), ())), preferred_element_type=jnp.float32
        )
        return join(sums, 2) * factor - shift

    convert(0)

    def multiply_send(i, carry):
        convert(i + 1)
        send_ref[i] = partial(i).astype(send_ref.dtype)
        return carry

    def multiply_keep(i, carry):
        convert(half + i + 1)
        keep_ref[i] = partial(half + i).astype(keep_ref.dtype)
        return carry

    lax.fori_loop(0, half, multiply_send, 0, unroll=True)
    lax.fori_loop(0, half - 1, multiply_keep, 0, unroll=True)
    keep_ref[half - 1] = partial(blocks - 1).astype(keep_ref.dtype)
    for t in range(tails):
        fetch_noise(t).wait()
        tail_ref[t] = light * noise_ref[t].astype(jnp.float32)


def scan_pieces(order, held_ref, pieces):
    values = [piece[j].astype(jnp.float32) for piece in pieces for j in range(piece.shape[0])]
    largest = jnp.abs(values[0])
    column = values[0]
    for value in values[1:]:
        largest = jnp.maximum(largest, jnp.abs(value))
        column = column + value
    scale = row_scale(largest)
    total = None
    for i, value in enumerate(values):
        part = jnp.dot(
            split(value * scale, 2), held_ref[order[i]], preferred_element_type=jnp.float32
        )
        total = part if total is None else total + part
    return join(total, 2) / scale, jnp.sum(column, axis=1, keepdims=True)


def early_kernel(order, held_ref, *refs):
    pieces = refs[:-2]
    total_ref, column_ref = refs[-2:]
    total, column = scan_pieces(order, held_ref, pieces)
    total_ref[...] = total
    column_ref[...] = jnp.broadcast_to(column, column_ref.shape)


def late_kernel(order, scale_back, held_ref, means_ref, scales_ref, own_ref, *refs):
    early_ref, early_column_ref = refs[:2]
    pieces = refs[2:-2]
    phen_ref, out_ref = refs[-2:]
    phen_ref[...] = own_ref[0]
    total, column = scan_pieces(order, held_ref, pieces)
    total = total + early_ref[...]
    column = column + early_column_ref[:, :1]
    if scale_back is None:
        out_ref[...] = total
    else:
        out_ref[...] = (total - column * means_ref[...]) / (scales_ref[...] * scale_back)


def on_device(genotypes, means, scales, causal, effects, heritability, noise):
    samples, variants = genotypes.shape
    pheno, causal_count = causal.shape
    blocks = lax.axis_size("var")
    samp = lax.axis_size("samp")
    share = samples // blocks
    bits = blocks.bit_length() - 1
    if blocks != 1 << bits or bits < 3:
        raise ValueError("var size")
    tails = blocks // 8

    half = blocks // 2

    def relative_of(i):
        core = 1 - i // half
        group = (i % half // tails + 1) % 4
        return core + 2 * group + 8 * (i % tails)

    def position(core, group, tail):
        return (1 - core) * half + (group + 3) % 4 * tails + tail

    def pairs(k):
        return [(i, i ^ k) for i in range(blocks)]

    vmem = pl.BlockSpec(memory_space=pltpu.VMEM)
    hbm = pl.BlockSpec(memory_space=pltpu.HBM)
    means_row = means[None, :]
    scales_row = scales[None, :]
    width = -(-causal_count // LANES) * LANES

    held, send, keep, tail = pl.pallas_call(
        lambda *refs: evolve_kernel(blocks, share, FLIGHT, relative_of, *refs),
        out_shape=(
            jax.ShapeDtypeStruct((blocks, share, variants), SMALL),
            jax.ShapeDtypeStruct((half, pheno, share), jnp.bfloat16),
            jax.ShapeDtypeStruct((half, pheno, share), jnp.float32),
            jax.ShapeDtypeStruct((tails, pheno, share), jnp.float32),
        ),
        in_specs=[hbm] * 7,
        out_specs=[vmem] * 4,
        scratch_shapes=[
            pltpu.VMEM((blocks, share, variants), genotypes.dtype),
            pltpu.VMEM((pheno, causal_count), jnp.int32),
            pltpu.VMEM((pheno, causal_count), jnp.float32),
            pltpu.VMEM((1, variants), jnp.float32),
            pltpu.VMEM((1, variants), jnp.float32),
            pltpu.VMEM((1, pheno), jnp.float32),
            pltpu.VMEM((pheno, width), jnp.int32),
            pltpu.VMEM((pheno, width), jnp.int32),
            pltpu.VMEM((pheno, width), jnp.float32),
            pltpu.VMEM((pheno, variants // LANES, LANES), jnp.float32),
            pltpu.VMEM((pheno, variants), jnp.float32),
            pltpu.VMEM((tails, pheno, share), jnp.bfloat16),
            pltpu.SemaphoreType.DMA((blocks,)),
            pltpu.SemaphoreType.DMA((tails,)),
            pltpu.SemaphoreType.DMA((5,)),
        ],
        compiler_params=pltpu.CompilerParams(vmem_limit_bytes=24 * MIB),
        name="evolve",
    )(
        *(
            pltpu.with_memory_space_constraint(x, pltpu.HBM)
            for x in (
                genotypes,
                noise,
                means_row,
                scales_row,
                causal,
                effects,
                heritability[None, :],
            )
        )
    )

    got = lax.ppermute(send, "var", pairs(1))
    chip = [
        keep[i * tails : (i + 1) * tails] + got[i * tails : (i + 1) * tails].astype(jnp.float32)
        for i in range(4)
    ]
    arrived = [
        lax.ppermute(chip[g - 1].astype(jnp.bfloat16), "var", pairs(2 * g)) for g in (1, 2, 3)
    ]
    total = chip[3]
    for other in arrived:
        total = total + other.astype(jnp.float32)

    step = 1
    while step < tails:
        mine = total.astype(jnp.bfloat16)
        other = lax.ppermute(mine, "var", pairs(8 * step))
        other = jnp.concatenate([other[t ^ step][None] for t in range(tails)], axis=0)
        total = mine.astype(jnp.float32) + other.astype(jnp.float32)
        step *= 2

    own = (total + tail).astype(jnp.bfloat16)
    groups = {0: own}
    for g in (1, 2, 3):
        groups[g] = lax.ppermute(own, "var", pairs(2 * g))
    others = {g: lax.ppermute(groups[g], "var", pairs(1)) for g in range(4)}
    first = [(0, g, groups[g]) for g in range(4)] + [(1, g, others[g]) for g in (0, 3, 2)]
    last = [(1, 1, others[1])]

    def places(chosen):
        return [position(core, g, t) for core, g, _ in chosen for t in range(tails)]

    def arrays(chosen):
        return [array for _, _, array in chosen]

    alone = samp == 1
    total_samples = jnp.float32(samples * samp)
    scale_back = float(samples * samp) ** 0.5 if alone else None
    params = pltpu.CompilerParams(vmem_limit_bytes=8 * MIB)
    early, early_column = pl.pallas_call(
        lambda *refs: early_kernel(places(first), *refs),
        out_shape=(
            jax.ShapeDtypeStruct((pheno, variants), jnp.float32),
            jax.ShapeDtypeStruct((pheno, LANES), jnp.float32),
        ),
        in_specs=[vmem] * (1 + len(first)),
        out_specs=[vmem] * 2,
        compiler_params=params,
        name="scan_early",
    )(held, *arrays(first))
    phen_out, scores = pl.pallas_call(
        lambda *refs: late_kernel(places(last), scale_back, *refs),
        out_shape=(
            jax.ShapeDtypeStruct((pheno, share), jnp.bfloat16),
            jax.ShapeDtypeStruct((pheno, variants), jnp.float32),
        ),
        in_specs=[vmem] * (6 + len(last)),
        out_specs=[vmem] * 2,
        compiler_params=params,
        name="scan_late",
    )(held, means_row, scales_row, own, early, early_column, *arrays(last))
    if alone:
        return phen_out, scores

    pieces = arrays(first + last)
    column = sum(jnp.sum(piece.astype(jnp.float32), axis=(0, 2)) for piece in pieces)
    score_width = variants // samp
    score_start = lax.axis_index("samp") * score_width
    means_part = lax.dynamic_slice_in_dim(means, score_start, score_width, 0)
    scales_part = lax.dynamic_slice_in_dim(scales, score_start, score_width, 0)
    column_sum = lax.psum(column, "samp")
    correction = column_sum[:, None] * means_part[None, :]
    summed = lax.psum_scatter(scores, "samp", scatter_dimension=1, tiled=True)
    scores = (summed - correction) / (scales_part[None, :] * jnp.sqrt(total_samples))
    return phen_out, scores


def solution(mesh):
    in_specs = (
        P("samp", "var"),
        P("var"),
        P("var"),
        P("rep", None),
        P("rep", None),
        P("rep"),
        P("rep", "samp"),
    )
    out_specs = (P("rep", ("samp", "var")), P("rep", ("var", "samp")))
    return jax.shard_map(
        on_device, mesh=mesh, in_specs=in_specs, out_specs=out_specs, check_vma=False
    )
```

```python
import jax
import jax.numpy as jnp
from jax import lax
from jax.experimental import pallas as pl
from jax.experimental.pallas import tpu as pltpu
from jax.sharding import PartitionSpec as P

LANES = 128
MIB = 1 << 20
SMALL = jnp.float8_e4m3fn
LARGEST = 448.0
FLIGHT = 3
CROSS = 1
SHIFT = 16.0
EFFECT_SCALE = 1024.0


def row_scale(values):
    largest = jnp.max(jnp.abs(values), axis=1, keepdims=True)
    scale = jnp.full_like(largest, 2.0**-30)
    for step in (32, 16, 8, 4, 2, 1):
        raised = scale * 2.0**step
        scale = jnp.where(largest * raised <= LARGEST, raised, scale)
    return scale


def split(values, count):
    parts = []
    for i in range(count):
        part = values.astype(SMALL)
        parts.append(part)
        if i + 1 < count:
            values = (values - part.astype(jnp.float32)) * SHIFT
    return jnp.concatenate(parts, axis=0)


def join(sums, count):
    rows = sums.shape[0] // count
    total = sums[(count - 1) * rows :]
    for i in reversed(range(count - 1)):
        total = sums[i * rows : (i + 1) * rows] + total * (1.0 / SHIFT)
    return total


def evolve_kernel(
    blocks,
    share,
    flight,
    relative_of,
    genotypes_hbm,
    noise_hbm,
    means_hbm,
    scales_hbm,
    causal_hbm,
    effects_hbm,
    heritability_hbm,
    held_ref,
    send_ref,
    keep_ref,
    tail_ref,
    staged_ref,
    causal_ref,
    effects_ref,
    means_ref,
    scales_ref,
    heritability_ref,
    high_ref,
    low_ref,
    value_ref,
    beta_ref,
    weight_ref,
    noise_ref,
    block_sem,
    noise_sem,
    small_sem,
):
    pheno, variants = weight_ref.shape
    me = lax.axis_index("var")
    tails = tail_ref.shape[0]
    half = blocks // 2

    def fetch(i):
        start = pl.multiple_of((me ^ relative_of(i, me)) * share, share)
        return pltpu.make_async_copy(
            genotypes_hbm.at[pl.ds(start, share), :], staged_ref.at[i], block_sem.at[i]
        )

    def fetch_noise(t):
        start = pl.multiple_of((me ^ relative_of(blocks - tails + t, me)) * share, share)
        return pltpu.make_async_copy(
            noise_hbm.at[:, pl.ds(start, share)], noise_ref.at[t], noise_sem.at[t]
        )

    small = [
        pltpu.make_async_copy(source, target, small_sem.at[i])
        for i, (source, target) in enumerate(
            (
                (causal_hbm, causal_ref),
                (effects_hbm, effects_ref),
                (scales_hbm, scales_ref),
                (means_hbm, means_ref),
                (heritability_hbm, heritability_ref),
            )
        )
    ]
    for copy in small:
        copy.start()
    for t in range(tails):
        fetch_noise(t).start()

    causal_count = causal_ref.shape[1]
    high_count = variants // LANES
    high_ref[...] = jnp.full(high_ref.shape, -1, jnp.int32)
    low_ref[...] = jnp.zeros(low_ref.shape, jnp.int32)
    value_ref[...] = jnp.zeros(value_ref.shape, jnp.float32)
    for copy in small[:2]:
        copy.wait()
    for i in range(flight):
        fetch(i).start()
    local = causal_ref[...] - me * variants
    inside = (local >= 0) & (local < variants)
    high_ref[:, :causal_count] = jnp.where(inside, local // LANES, -1)
    low_ref[:, :causal_count] = jnp.where(inside, local % LANES, 0)
    value_ref[:, :causal_count] = effects_ref[...] * EFFECT_SCALE
    width = high_ref.shape[1]
    high_iota = lax.broadcasted_iota(jnp.int32, (high_count, width), 0)
    low_iota = lax.broadcasted_iota(jnp.int32, (LANES, width), 0).astype(jnp.int16)

    def build(p):
        row = pl.ds(p, 1)
        value = jnp.where(high_ref[row, :] == high_iota, value_ref[row, :], 0.0)
        low = jnp.broadcast_to(low_ref[row, :], (LANES, width)).astype(jnp.int16)
        hits = jnp.where(low == low_iota, jnp.bfloat16(1), jnp.bfloat16(0)).astype(SMALL)
        sums = lax.dot_general(
            split(value, 4), hits, (((1,), (1,)), ((), ())), preferred_element_type=jnp.float32
        )
        beta_ref[p] = join(sums, 4) * (1.0 / EFFECT_SCALE)

    steps = half
    per_step = -(-pheno // steps)

    def build_step(i, carry):
        @pl.when(flight + i < blocks)
        def _():
            fetch(flight + i).start()

        for j in range(per_step):
            build(jnp.minimum(i * per_step + j, pheno - 1))
        return carry

    lax.fori_loop(0, steps, build_step, 0, unroll=True)
    for i in range(flight + steps, blocks):
        fetch(i).start()

    for copy in small[2:]:
        copy.wait()
    offset = jnp.zeros((pheno, LANES), jnp.float32)
    for h in range(high_count):
        lanes = slice(h * LANES, (h + 1) * LANES)
        weight = (beta_ref[:, h, :] / scales_ref[:, lanes]).astype(jnp.bfloat16)
        weight = weight.astype(jnp.float32)
        weight_ref[:, lanes] = weight
        offset += weight * means_ref[:, lanes]
    offset = jnp.sum(offset, axis=1, keepdims=True)

    square = (pheno, pheno)
    diagonal = lax.broadcasted_iota(jnp.int32, square, 0) == lax.broadcasted_iota(
        jnp.int32, square, 1
    )
    share_genetic = jnp.sum(
        jnp.where(diagonal, jnp.broadcast_to(heritability_ref[...], square), 0.0),
        axis=1,
        keepdims=True,
    )
    heavy = jnp.sqrt(share_genetic)
    light = jnp.sqrt(1.0 - share_genetic)
    scale = row_scale(weight_ref[...])
    weights = split(weight_ref[...] * scale, 2)
    factor = heavy / scale
    shift = heavy * offset

    def convert(i):
        fetch(i).wait()
        held_ref[i] = staged_ref[i].astype(SMALL)

    def partial(i):
        sums = lax.dot_general(
            weights, held_ref[i], (((1,), (1,)), ((), ())), preferred_element_type=jnp.float32
        )
        return join(sums, 2) * factor - shift

    convert(0)

    def multiply_send(i, carry):
        convert(i + 1)
        send_ref[i] = partial(i).astype(send_ref.dtype)
        return carry

    def multiply_keep(i, carry):
        convert(half + i + 1)
        keep_ref[i] = partial(half + i).astype(keep_ref.dtype)
        return carry

    lax.fori_loop(0, half, multiply_send, 0, unroll=True)
    lax.fori_loop(0, half - 1, multiply_keep, 0, unroll=True)
    keep_ref[half - 1] = partial(blocks - 1).astype(keep_ref.dtype)
    for t in range(tails):
        fetch_noise(t).wait()
        tail_ref[t] = light * noise_ref[t].astype(jnp.float32)


def scan_pieces(order, held_ref, pieces):
    values = [piece[j].astype(jnp.float32) for piece in pieces for j in range(piece.shape[0])]
    largest = jnp.abs(values[0])
    column = values[0]
    for value in values[1:]:
        largest = jnp.maximum(largest, jnp.abs(value))
        column = column + value
    scale = row_scale(largest)
    total = None
    for i, value in enumerate(values):
        part = jnp.dot(
            split(value * scale, 2), held_ref[order[i]], preferred_element_type=jnp.float32
        )
        total = part if total is None else total + part
    return join(total, 2) / scale, jnp.sum(column, axis=1, keepdims=True)


def early_kernel(order, held_ref, *refs):
    pieces = refs[:-2]
    total_ref, column_ref = refs[-2:]
    total, column = scan_pieces(order, held_ref, pieces)
    total_ref[...] = total
    column_ref[...] = jnp.broadcast_to(column, column_ref.shape)


def late_kernel(
    order, scale_back, swapped, held_ref, means_ref, scales_ref, own_ref, other_ref, *refs
):
    early_ref, early_column_ref = refs[:2]
    pieces = refs[2:-2]
    phen_ref, out_ref = refs[-2:]
    mine = swapped(lax.axis_index("var")) == 0
    phen_ref[...] = jnp.where(mine, own_ref[0], other_ref[0])
    total, column = scan_pieces(order, held_ref, pieces)
    total = total + early_ref[...]
    column = column + early_column_ref[:, :1]
    if scale_back is None:
        out_ref[...] = total
    else:
        out_ref[...] = (total - column * means_ref[...]) / (scales_ref[...] * scale_back)


def on_device(genotypes, means, scales, causal, effects, heritability, noise):
    samples, variants = genotypes.shape
    pheno, causal_count = causal.shape
    blocks = lax.axis_size("var")
    samp = lax.axis_size("samp")
    share = samples // blocks
    bits = blocks.bit_length() - 1
    if blocks != 1 << bits or bits < 3:
        raise ValueError("var size")
    tails = blocks // 8

    half = blocks // 2

    def parity(chip):
        total = 0
        for bit in range(bits - 1):
            if CROSS >> bit & 1:
                total = total ^ (chip >> bit & 1)
        return total

    def relative_of(i, me):
        core = 1 - i // half
        group = (i % half // tails + 1) % 4
        return (core ^ parity(me >> 1)) + 2 * group + 8 * (i % tails)

    def position(core, group, tail):
        return (1 - core) * half + (group + 3) % 4 * tails + tail

    def pairs(k):
        return [(i, i ^ k ^ parity(k >> 1)) for i in range(blocks)]

    vmem = pl.BlockSpec(memory_space=pltpu.VMEM)
    hbm = pl.BlockSpec(memory_space=pltpu.HBM)
    means_row = means[None, :]
    scales_row = scales[None, :]
    width = -(-causal_count // LANES) * LANES

    held, send, keep, tail = pl.pallas_call(
        lambda *refs: evolve_kernel(blocks, share, FLIGHT, relative_of, *refs),
        out_shape=(
            jax.ShapeDtypeStruct((blocks, share, variants), SMALL),
            jax.ShapeDtypeStruct((half, pheno, share), jnp.bfloat16),
            jax.ShapeDtypeStruct((half, pheno, share), jnp.float32),
            jax.ShapeDtypeStruct((tails, pheno, share), jnp.float32),
        ),
        in_specs=[hbm] * 7,
        out_specs=[vmem] * 4,
        scratch_shapes=[
            pltpu.VMEM((blocks, share, variants), genotypes.dtype),
            pltpu.VMEM((pheno, causal_count), jnp.int32),
            pltpu.VMEM((pheno, causal_count), jnp.float32),
            pltpu.VMEM((1, variants), jnp.float32),
            pltpu.VMEM((1, variants), jnp.float32),
            pltpu.VMEM((1, pheno), jnp.float32),
            pltpu.VMEM((pheno, width), jnp.int32),
            pltpu.VMEM((pheno, width), jnp.int32),
            pltpu.VMEM((pheno, width), jnp.float32),
            pltpu.VMEM((pheno, variants // LANES, LANES), jnp.float32),
            pltpu.VMEM((pheno, variants), jnp.float32),
            pltpu.VMEM((tails, pheno, share), jnp.bfloat16),
            pltpu.SemaphoreType.DMA((blocks,)),
            pltpu.SemaphoreType.DMA((tails,)),
            pltpu.SemaphoreType.DMA((5,)),
        ],
        compiler_params=pltpu.CompilerParams(vmem_limit_bytes=24 * MIB),
        name="evolve",
    )(
        *(
            pltpu.with_memory_space_constraint(x, pltpu.HBM)
            for x in (
                genotypes,
                noise,
                means_row,
                scales_row,
                causal,
                effects,
                heritability[None, :],
            )
        )
    )

    got = lax.ppermute(send, "var", pairs(1))
    chip = [
        keep[i * tails : (i + 1) * tails] + got[i * tails : (i + 1) * tails].astype(jnp.float32)
        for i in range(4)
    ]
    arrived = [
        lax.ppermute(chip[g - 1].astype(jnp.bfloat16), "var", pairs(2 * g)) for g in (1, 2, 3)
    ]
    total = chip[3]
    for other in arrived:
        total = total + other.astype(jnp.float32)

    step = 1
    while step < tails:
        mine = total.astype(jnp.bfloat16)
        other = lax.ppermute(mine, "var", pairs(8 * step))
        other = jnp.concatenate([other[t ^ step][None] for t in range(tails)], axis=0)
        total = mine.astype(jnp.float32) + other.astype(jnp.float32)
        step *= 2

    own = (total + tail).astype(jnp.bfloat16)
    groups = {0: own}
    for g in (1, 2, 3):
        groups[g] = lax.ppermute(own, "var", pairs(2 * g))
    others = {g: lax.ppermute(groups[g], "var", pairs(1)) for g in range(4)}
    first = [(0, g, groups[g]) for g in range(4)] + [(1, g, others[g]) for g in (0, 3, 2)]
    last = [(1, 1, others[1])]

    def places(chosen):
        return [position(core, g, t) for core, g, _ in chosen for t in range(tails)]

    def arrays(chosen):
        return [array for _, _, array in chosen]

    alone = samp == 1
    total_samples = jnp.float32(samples * samp)
    scale_back = float(samples * samp) ** 0.5 if alone else None
    params = pltpu.CompilerParams(vmem_limit_bytes=8 * MIB)
    early, early_column = pl.pallas_call(
        lambda *refs: early_kernel(places(first), *refs),
        out_shape=(
            jax.ShapeDtypeStruct((pheno, variants), jnp.float32),
            jax.ShapeDtypeStruct((pheno, LANES), jnp.float32),
        ),
        in_specs=[vmem] * (1 + len(first)),
        out_specs=[vmem] * 2,
        compiler_params=params,
        name="scan_early",
    )(held, *arrays(first))
    phen_out, scores = pl.pallas_call(
        lambda *refs: late_kernel(
            places(last), scale_back, lambda me: parity(me >> 1), *refs
        ),
        out_shape=(
            jax.ShapeDtypeStruct((pheno, share), jnp.bfloat16),
            jax.ShapeDtypeStruct((pheno, variants), jnp.float32),
        ),
        in_specs=[vmem] * (7 + len(last)),
        out_specs=[vmem] * 2,
        compiler_params=params,
        name="scan_late",
    )(held, means_row, scales_row, own, others[0], early, early_column, *arrays(last))
    if alone:
        return phen_out, scores

    pieces = arrays(first + last)
    column = sum(jnp.sum(piece.astype(jnp.float32), axis=(0, 2)) for piece in pieces)
    score_width = variants // samp
    score_start = lax.axis_index("samp") * score_width
    means_part = lax.dynamic_slice_in_dim(means, score_start, score_width, 0)
    scales_part = lax.dynamic_slice_in_dim(scales, score_start, score_width, 0)
    column_sum = lax.psum(column, "samp")
    correction = column_sum[:, None] * means_part[None, :]
    summed = lax.psum_scatter(scores, "samp", scatter_dimension=1, tiled=True)
    scores = (summed - correction) / (scales_part[None, :] * jnp.sqrt(total_samples))
    return phen_out, scores


def solution(mesh):
    in_specs = (
        P("samp", "var"),
        P("var"),
        P("var"),
        P("rep", None),
        P("rep", None),
        P("rep"),
        P("rep", "samp"),
    )
    out_specs = (P("rep", ("samp", "var")), P("rep", ("var", "samp")))
    return jax.shard_map(
        on_device, mesh=mesh, in_specs=in_specs, out_specs=out_specs, check_vma=False
    )
```

```python
import jax
import jax.numpy as jnp
from jax import lax
from jax.experimental import pallas as pl
from jax.experimental.pallas import tpu as pltpu
from jax.sharding import PartitionSpec as P

LANES = 128
MIB = 1 << 20
SMALL = jnp.float8_e4m3fn
LARGEST = 448.0
FLIGHT = 3
CROSS = 1
SHIFT = 16.0
EFFECT_SCALE = 1024.0


def row_scale(values):
    largest = jnp.max(jnp.abs(values), axis=1, keepdims=True)
    scale = jnp.full_like(largest, 2.0**-30)
    for step in (32, 16, 8, 4, 2, 1):
        raised = scale * 2.0**step
        scale = jnp.where(largest * raised <= LARGEST, raised, scale)
    return scale


def split(values, count):
    parts = []
    for i in range(count):
        part = values.astype(SMALL)
        parts.append(part)
        if i + 1 < count:
            values = (values - part.astype(jnp.float32)) * SHIFT
    return jnp.concatenate(parts, axis=0)


def join(sums, count):
    rows = sums.shape[0] // count
    total = sums[(count - 1) * rows :]
    for i in reversed(range(count - 1)):
        total = sums[i * rows : (i + 1) * rows] + total * (1.0 / SHIFT)
    return total


def evolve_kernel(
    blocks,
    share,
    flight,
    relative_of,
    genotypes_hbm,
    noise_hbm,
    means_hbm,
    scales_hbm,
    causal_hbm,
    effects_hbm,
    heritability_hbm,
    held_ref,
    send_ref,
    keep_ref,
    tail_ref,
    staged_ref,
    causal_ref,
    effects_ref,
    means_ref,
    scales_ref,
    heritability_ref,
    high_ref,
    low_ref,
    value_ref,
    beta_ref,
    weight_ref,
    noise_ref,
    block_sem,
    noise_sem,
    small_sem,
):
    pheno, variants = weight_ref.shape
    me = lax.axis_index("var")
    tails = tail_ref.shape[0]
    half = blocks // 2

    def fetch(i):
        start = pl.multiple_of((me ^ relative_of(i, me)) * share, share)
        return pltpu.make_async_copy(
            genotypes_hbm.at[pl.ds(start, share), :], staged_ref.at[i], block_sem.at[i]
        )

    def fetch_noise(t):
        start = pl.multiple_of((me ^ relative_of(blocks - tails + t, me)) * share, share)
        return pltpu.make_async_copy(
            noise_hbm.at[:, pl.ds(start, share)], noise_ref.at[t], noise_sem.at[t]
        )

    small = [
        pltpu.make_async_copy(source, target, small_sem.at[i])
        for i, (source, target) in enumerate(
            (
                (causal_hbm, causal_ref),
                (effects_hbm, effects_ref),
                (scales_hbm, scales_ref),
                (means_hbm, means_ref),
                (heritability_hbm, heritability_ref),
            )
        )
    ]
    for copy in small:
        copy.start()
    for t in range(tails):
        fetch_noise(t).start()

    causal_count = causal_ref.shape[1]
    high_count = variants // LANES
    high_ref[...] = jnp.full(high_ref.shape, -1, jnp.int32)
    low_ref[...] = jnp.zeros(low_ref.shape, jnp.int32)
    value_ref[...] = jnp.zeros(value_ref.shape, jnp.float32)
    for copy in small[:2]:
        copy.wait()
    for i in range(flight):
        fetch(i).start()
    local = causal_ref[...] - me * variants
    inside = (local >= 0) & (local < variants)
    high_ref[:, :causal_count] = jnp.where(inside, local // LANES, -1)
    low_ref[:, :causal_count] = jnp.where(inside, local % LANES, 0)
    value_ref[:, :causal_count] = effects_ref[...] * EFFECT_SCALE
    width = high_ref.shape[1]
    high_iota = lax.broadcasted_iota(jnp.int32, (high_count, width), 0)
    low_iota = lax.broadcasted_iota(jnp.int32, (LANES, width), 0).astype(jnp.int16)

    def build(p):
        row = pl.ds(p, 1)
        value = jnp.where(high_ref[row, :] == high_iota, value_ref[row, :], 0.0)
        low = jnp.broadcast_to(low_ref[row, :], (LANES, width)).astype(jnp.int16)
        hits = jnp.where(low == low_iota, jnp.bfloat16(1), jnp.bfloat16(0)).astype(SMALL)
        sums = lax.dot_general(
            split(value, 4), hits, (((1,), (1,)), ((), ())), preferred_element_type=jnp.float32
        )
        beta_ref[p] = join(sums, 4) * (1.0 / EFFECT_SCALE)

    steps = half
    per_step = -(-pheno // steps)

    def build_step(i, carry):
        @pl.when(flight + i < blocks)
        def _():
            fetch(flight + i).start()

        for j in range(per_step):
            build(jnp.minimum(i * per_step + j, pheno - 1))
        return carry

    lax.fori_loop(0, steps, build_step, 0, unroll=True)
    for i in range(flight + steps, blocks):
        fetch(i).start()

    for copy in small[2:]:
        copy.wait()
    offset = jnp.zeros((pheno, LANES), jnp.float32)
    for h in range(high_count):
        lanes = slice(h * LANES, (h + 1) * LANES)
        weight = (beta_ref[:, h, :] / scales_ref[:, lanes]).astype(jnp.bfloat16)
        weight = weight.astype(jnp.float32)
        weight_ref[:, lanes] = weight
        offset += weight * means_ref[:, lanes]
    offset = jnp.sum(offset, axis=1, keepdims=True)

    square = (pheno, pheno)
    diagonal = lax.broadcasted_iota(jnp.int32, square, 0) == lax.broadcasted_iota(
        jnp.int32, square, 1
    )
    share_genetic = jnp.sum(
        jnp.where(diagonal, jnp.broadcast_to(heritability_ref[...], square), 0.0),
        axis=1,
        keepdims=True,
    )
    heavy = jnp.sqrt(share_genetic)
    light = jnp.sqrt(1.0 - share_genetic)
    scale = row_scale(weight_ref[...])
    weights = split(weight_ref[...] * scale, 2)
    factor = heavy / scale
    shift = heavy * offset

    for start in range(0, blocks, 2):
        for i in (start, start + 1):
            fetch(i).wait()
        for i in (start, start + 1):
            block = staged_ref[i].astype(SMALL)
            held_ref[i] = block
            sums = lax.dot_general(
                weights, block, (((1,), (1,)), ((), ())), preferred_element_type=jnp.float32
            )
            value = join(sums, 2) * factor - shift
            if i < half:
                send_ref[i] = value.astype(send_ref.dtype)
            else:
                keep_ref[i - half] = value.astype(keep_ref.dtype)
    for t in range(tails):
        fetch_noise(t).wait()
        tail_ref[t] = light * noise_ref[t].astype(jnp.float32)


def scan_pieces(order, held_ref, pieces):
    values = [piece[j].astype(jnp.float32) for piece in pieces for j in range(piece.shape[0])]
    largest = jnp.abs(values[0])
    column = values[0]
    for value in values[1:]:
        largest = jnp.maximum(largest, jnp.abs(value))
        column = column + value
    scale = row_scale(largest)
    total = None
    for i, value in enumerate(values):
        part = jnp.dot(
            split(value * scale, 2), held_ref[order[i]], preferred_element_type=jnp.float32
        )
        total = part if total is None else total + part
    return join(total, 2) / scale, jnp.sum(column, axis=1, keepdims=True)


def early_kernel(order, held_ref, *refs):
    pieces = refs[:-2]
    total_ref, column_ref = refs[-2:]
    total, column = scan_pieces(order, held_ref, pieces)
    total_ref[...] = total
    column_ref[...] = jnp.broadcast_to(column, column_ref.shape)


def late_kernel(
    order, scale_back, swapped, held_ref, means_ref, scales_ref, own_ref, other_ref, *refs
):
    early_ref, early_column_ref = refs[:2]
    pieces = refs[2:-2]
    phen_ref, out_ref = refs[-2:]
    mine = swapped(lax.axis_index("var")) == 0
    phen_ref[...] = jnp.where(mine, own_ref[0], other_ref[0])
    total, column = scan_pieces(order, held_ref, pieces)
    total = total + early_ref[...]
    column = column + early_column_ref[:, :1]
    if scale_back is None:
        out_ref[...] = total
    else:
        out_ref[...] = (total - column * means_ref[...]) / (scales_ref[...] * scale_back)


def on_device(genotypes, means, scales, causal, effects, heritability, noise):
    samples, variants = genotypes.shape
    pheno, causal_count = causal.shape
    blocks = lax.axis_size("var")
    samp = lax.axis_size("samp")
    share = samples // blocks
    bits = blocks.bit_length() - 1
    if blocks != 1 << bits or bits < 3:
        raise ValueError("var size")
    tails = blocks // 8

    half = blocks // 2

    def parity(chip):
        total = 0
        for bit in range(bits - 1):
            if CROSS >> bit & 1:
                total = total ^ (chip >> bit & 1)
        return total

    def relative_of(i, me):
        core = 1 - i // half
        group = (i % half // tails + 1) % 4
        return (core ^ parity(me >> 1)) + 2 * group + 8 * (i % tails)

    def position(core, group, tail):
        return (1 - core) * half + (group + 3) % 4 * tails + tail

    def pairs(k):
        return [(i, i ^ k ^ parity(k >> 1)) for i in range(blocks)]

    vmem = pl.BlockSpec(memory_space=pltpu.VMEM)
    hbm = pl.BlockSpec(memory_space=pltpu.HBM)
    means_row = means[None, :]
    scales_row = scales[None, :]
    width = -(-causal_count // LANES) * LANES

    held, send, keep, tail = pl.pallas_call(
        lambda *refs: evolve_kernel(blocks, share, FLIGHT, relative_of, *refs),
        out_shape=(
            jax.ShapeDtypeStruct((blocks, share, variants), SMALL),
            jax.ShapeDtypeStruct((half, pheno, share), jnp.bfloat16),
            jax.ShapeDtypeStruct((half, pheno, share), jnp.float32),
            jax.ShapeDtypeStruct((tails, pheno, share), jnp.float32),
        ),
        in_specs=[hbm] * 7,
        out_specs=[vmem] * 4,
        scratch_shapes=[
            pltpu.VMEM((blocks, share, variants), genotypes.dtype),
            pltpu.VMEM((pheno, causal_count), jnp.int32),
            pltpu.VMEM((pheno, causal_count), jnp.float32),
            pltpu.VMEM((1, variants), jnp.float32),
            pltpu.VMEM((1, variants), jnp.float32),
            pltpu.VMEM((1, pheno), jnp.float32),
            pltpu.VMEM((pheno, width), jnp.int32),
            pltpu.VMEM((pheno, width), jnp.int32),
            pltpu.VMEM((pheno, width), jnp.float32),
            pltpu.VMEM((pheno, variants // LANES, LANES), jnp.float32),
            pltpu.VMEM((pheno, variants), jnp.float32),
            pltpu.VMEM((tails, pheno, share), jnp.bfloat16),
            pltpu.SemaphoreType.DMA((blocks,)),
            pltpu.SemaphoreType.DMA((tails,)),
            pltpu.SemaphoreType.DMA((5,)),
        ],
        compiler_params=pltpu.CompilerParams(vmem_limit_bytes=24 * MIB),
        name="evolve",
    )(
        *(
            pltpu.with_memory_space_constraint(x, pltpu.HBM)
            for x in (
                genotypes,
                noise,
                means_row,
                scales_row,
                causal,
                effects,
                heritability[None, :],
            )
        )
    )

    got = lax.ppermute(send, "var", pairs(1))
    chip = [
        keep[i * tails : (i + 1) * tails] + got[i * tails : (i + 1) * tails].astype(jnp.float32)
        for i in range(4)
    ]
    arrived = [
        lax.ppermute(chip[g - 1].astype(jnp.bfloat16), "var", pairs(2 * g)) for g in (1, 2, 3)
    ]
    total = chip[3]
    for other in arrived:
        total = total + other.astype(jnp.float32)

    step = 1
    while step < tails:
        mine = total.astype(jnp.bfloat16)
        other = lax.ppermute(mine, "var", pairs(8 * step))
        other = jnp.concatenate([other[t ^ step][None] for t in range(tails)], axis=0)
        total = mine.astype(jnp.float32) + other.astype(jnp.float32)
        step *= 2

    own = (total + tail).astype(jnp.bfloat16)
    groups = {0: own}
    for g in (1, 2, 3):
        groups[g] = lax.ppermute(own, "var", pairs(2 * g))
    others = {g: lax.ppermute(groups[g], "var", pairs(1)) for g in range(4)}
    first = [(0, g, groups[g]) for g in range(4)] + [(1, g, others[g]) for g in (0, 3, 2)]
    last = [(1, 1, others[1])]

    def places(chosen):
        return [position(core, g, t) for core, g, _ in chosen for t in range(tails)]

    def arrays(chosen):
        return [array for _, _, array in chosen]

    alone = samp == 1
    total_samples = jnp.float32(samples * samp)
    scale_back = float(samples * samp) ** 0.5 if alone else None
    params = pltpu.CompilerParams(vmem_limit_bytes=8 * MIB)
    early, early_column = pl.pallas_call(
        lambda *refs: early_kernel(places(first), *refs),
        out_shape=(
            jax.ShapeDtypeStruct((pheno, variants), jnp.float32),
            jax.ShapeDtypeStruct((pheno, LANES), jnp.float32),
        ),
        in_specs=[vmem] * (1 + len(first)),
        out_specs=[vmem] * 2,
        compiler_params=params,
        name="scan_early",
    )(held, *arrays(first))
    phen_out, scores = pl.pallas_call(
        lambda *refs: late_kernel(
            places(last), scale_back, lambda me: parity(me >> 1), *refs
        ),
        out_shape=(
            jax.ShapeDtypeStruct((pheno, share), jnp.bfloat16),
            jax.ShapeDtypeStruct((pheno, variants), jnp.float32),
        ),
        in_specs=[vmem] * (7 + len(last)),
        out_specs=[vmem] * 2,
        compiler_params=params,
        name="scan_late",
    )(held, means_row, scales_row, own, others[0], early, early_column, *arrays(last))
    if alone:
        return phen_out, scores

    pieces = arrays(first + last)
    column = sum(jnp.sum(piece.astype(jnp.float32), axis=(0, 2)) for piece in pieces)
    score_width = variants // samp
    score_start = lax.axis_index("samp") * score_width
    means_part = lax.dynamic_slice_in_dim(means, score_start, score_width, 0)
    scales_part = lax.dynamic_slice_in_dim(scales, score_start, score_width, 0)
    column_sum = lax.psum(column, "samp")
    correction = column_sum[:, None] * means_part[None, :]
    summed = lax.psum_scatter(scores, "samp", scatter_dimension=1, tiled=True)
    scores = (summed - correction) / (scales_part[None, :] * jnp.sqrt(total_samples))
    return phen_out, scores


def solution(mesh):
    in_specs = (
        P("samp", "var"),
        P("var"),
        P("var"),
        P("rep", None),
        P("rep", None),
        P("rep"),
        P("rep", "samp"),
    )
    out_specs = (P("rep", ("samp", "var")), P("rep", ("var", "samp")))
    return jax.shard_map(
        on_device, mesh=mesh, in_specs=in_specs, out_specs=out_specs, check_vma=False
    )
```

```python
import jax
import jax.numpy as jnp
from jax import lax
from jax.experimental import pallas as pl
from jax.experimental.pallas import tpu as pltpu
from jax.sharding import PartitionSpec as P

LANES = 128
MIB = 1 << 20
SMALL = jnp.float8_e4m3fn
LARGEST = 448.0
EARLY = 2
FLIGHT = 3
CROSS = 1
SHIFT = 16.0
EFFECT_SCALE = 1024.0


def row_scale(values):
    largest = jnp.max(jnp.abs(values), axis=1, keepdims=True)
    scale = jnp.full_like(largest, 2.0**-30)
    for step in (32, 16, 8, 4, 2, 1):
        raised = scale * 2.0**step
        scale = jnp.where(largest * raised <= LARGEST, raised, scale)
    return scale


def split(values, count):
    parts = []
    for i in range(count):
        part = values.astype(SMALL)
        parts.append(part)
        if i + 1 < count:
            values = (values - part.astype(jnp.float32)) * SHIFT
    return jnp.concatenate(parts, axis=0)


def join(sums, count):
    rows = sums.shape[0] // count
    total = sums[(count - 1) * rows :]
    for i in reversed(range(count - 1)):
        total = sums[i * rows : (i + 1) * rows] + total * (1.0 / SHIFT)
    return total


def evolve_kernel(
    blocks,
    share,
    flight,
    relative_of,
    genotypes_hbm,
    noise_hbm,
    means_hbm,
    scales_hbm,
    causal_hbm,
    effects_hbm,
    heritability_hbm,
    held_ref,
    send_ref,
    keep_ref,
    tail_ref,
    staged_ref,
    causal_ref,
    effects_ref,
    means_ref,
    scales_ref,
    heritability_ref,
    high_ref,
    low_ref,
    value_ref,
    beta_ref,
    weight_ref,
    noise_ref,
    block_sem,
    noise_sem,
    small_sem,
):
    pheno, variants = weight_ref.shape
    me = lax.axis_index("var")
    tails = tail_ref.shape[0]
    half = blocks // 2

    def fetch(i):
        start = pl.multiple_of((me ^ relative_of(i, me)) * share, share)
        return pltpu.make_async_copy(
            genotypes_hbm.at[pl.ds(start, share), :], staged_ref.at[i], block_sem.at[i]
        )

    def fetch_noise(t):
        start = pl.multiple_of((me ^ relative_of(blocks - tails + t, me)) * share, share)
        return pltpu.make_async_copy(
            noise_hbm.at[:, pl.ds(start, share)], noise_ref.at[t], noise_sem.at[t]
        )

    small = [
        pltpu.make_async_copy(source, target, small_sem.at[i])
        for i, (source, target) in enumerate(
            (
                (causal_hbm, causal_ref),
                (effects_hbm, effects_ref),
                (scales_hbm, scales_ref),
                (means_hbm, means_ref),
                (heritability_hbm, heritability_ref),
            )
        )
    ]
    for copy in small[:2]:
        copy.start()
    for i in range(EARLY):
        fetch(i).start()
    for copy in small[2:]:
        copy.start()
    for t in range(tails):
        fetch_noise(t).start()

    causal_count = causal_ref.shape[1]
    high_count = variants // LANES
    high_ref[...] = jnp.full(high_ref.shape, -1, jnp.int32)
    low_ref[...] = jnp.zeros(low_ref.shape, jnp.int32)
    value_ref[...] = jnp.zeros(value_ref.shape, jnp.float32)
    for copy in small[:2]:
        copy.wait()
    for i in range(EARLY, flight):
        fetch(i).start()
    local = causal_ref[...] - me * variants
    inside = (local >= 0) & (local < variants)
    high_ref[:, :causal_count] = jnp.where(inside, local // LANES, -1)
    low_ref[:, :causal_count] = jnp.where(inside, local % LANES, 0)
    value_ref[:, :causal_count] = effects_ref[...] * EFFECT_SCALE
    width = high_ref.shape[1]
    high_iota = lax.broadcasted_iota(jnp.int32, (high_count, width), 0)
    low_iota = lax.broadcasted_iota(jnp.int32, (LANES, width), 0).astype(jnp.int16)

    def build(p):
        row = pl.ds(p, 1)
        value = jnp.where(high_ref[row, :] == high_iota, value_ref[row, :], 0.0)
        low = jnp.broadcast_to(low_ref[row, :], (LANES, width)).astype(jnp.int16)
        hits = jnp.where(low == low_iota, jnp.bfloat16(1), jnp.bfloat16(0)).astype(SMALL)
        sums = lax.dot_general(
            split(value, 4), hits, (((1,), (1,)), ((), ())), preferred_element_type=jnp.float32
        )
        beta_ref[p] = join(sums, 4) * (1.0 / EFFECT_SCALE)

    steps = half
    per_step = -(-pheno // steps)

    def build_step(i, carry):
        @pl.when(flight + i < blocks)
        def _():
            fetch(flight + i).start()

        for j in range(per_step):
            build(jnp.minimum(i * per_step + j, pheno - 1))
        return carry

    lax.fori_loop(0, steps, build_step, 0, unroll=True)
    for i in range(flight + steps, blocks):
        fetch(i).start()

    for copy in small[2:]:
        copy.wait()
    offset = jnp.zeros((pheno, LANES), jnp.float32)
    for h in range(high_count):
        lanes = slice(h * LANES, (h + 1) * LANES)
        weight = (beta_ref[:, h, :] / scales_ref[:, lanes]).astype(jnp.bfloat16)
        weight = weight.astype(jnp.float32)
        weight_ref[:, lanes] = weight
        offset += weight * means_ref[:, lanes]
    offset = jnp.sum(offset, axis=1, keepdims=True)

    square = (pheno, pheno)
    diagonal = lax.broadcasted_iota(jnp.int32, square, 0) == lax.broadcasted_iota(
        jnp.int32, square, 1
    )
    share_genetic = jnp.sum(
        jnp.where(diagonal, jnp.broadcast_to(heritability_ref[...], square), 0.0),
        axis=1,
        keepdims=True,
    )
    heavy = jnp.sqrt(share_genetic)
    light = jnp.sqrt(1.0 - share_genetic)
    scale = row_scale(weight_ref[...])
    weights = split(weight_ref[...] * scale, 2)
    factor = heavy / scale
    shift = heavy * offset

    for start in range(0, blocks, 2):
        for i in (start, start + 1):
            fetch(i).wait()
        for i in (start, start + 1):
            block = staged_ref[i].astype(SMALL)
            held_ref[i] = block
            sums = lax.dot_general(
                weights, block, (((1,), (1,)), ((), ())), preferred_element_type=jnp.float32
            )
            value = join(sums, 2) * factor - shift
            if i < half:
                send_ref[i] = value.astype(send_ref.dtype)
            else:
                keep_ref[i - half] = value.astype(keep_ref.dtype)
    for t in range(tails):
        fetch_noise(t).wait()
        tail_ref[t] = light * noise_ref[t].astype(jnp.float32)


def scan_pieces(order, held_ref, pieces):
    values = [piece[j].astype(jnp.float32) for piece in pieces for j in range(piece.shape[0])]
    largest = jnp.abs(values[0])
    column = values[0]
    for value in values[1:]:
        largest = jnp.maximum(largest, jnp.abs(value))
        column = column + value
    scale = row_scale(largest)
    total = None
    for i, value in enumerate(values):
        part = jnp.dot(
            split(value * scale, 2), held_ref[order[i]], preferred_element_type=jnp.float32
        )
        total = part if total is None else total + part
    return join(total, 2) / scale, jnp.sum(column, axis=1, keepdims=True)


def early_kernel(order, held_ref, *refs):
    pieces = refs[:-2]
    total_ref, column_ref = refs[-2:]
    total, column = scan_pieces(order, held_ref, pieces)
    total_ref[...] = total
    column_ref[...] = jnp.broadcast_to(column, column_ref.shape)


def late_kernel(
    order, scale_back, swapped, held_ref, means_ref, scales_ref, own_ref, other_ref, *refs
):
    early_ref, early_column_ref = refs[:2]
    pieces = refs[2:-2]
    phen_ref, out_ref = refs[-2:]
    mine = swapped(lax.axis_index("var")) == 0
    phen_ref[...] = jnp.where(mine, own_ref[0], other_ref[0])
    total, column = scan_pieces(order, held_ref, pieces)
    total = total + early_ref[...]
    column = column + early_column_ref[:, :1]
    if scale_back is None:
        out_ref[...] = total
    else:
        out_ref[...] = (total - column * means_ref[...]) / (scales_ref[...] * scale_back)


def on_device(genotypes, means, scales, causal, effects, heritability, noise):
    samples, variants = genotypes.shape
    pheno, causal_count = causal.shape
    blocks = lax.axis_size("var")
    samp = lax.axis_size("samp")
    share = samples // blocks
    bits = blocks.bit_length() - 1
    if blocks != 1 << bits or bits < 3:
        raise ValueError("var size")
    tails = blocks // 8

    half = blocks // 2

    def parity(chip):
        total = 0
        for bit in range(bits - 1):
            if CROSS >> bit & 1:
                total = total ^ (chip >> bit & 1)
        return total

    def relative_of(i, me):
        core = 1 - i // half
        group = (i % half // tails + 1) % 4
        return (core ^ parity(me >> 1)) + 2 * group + 8 * (i % tails)

    def position(core, group, tail):
        return (1 - core) * half + (group + 3) % 4 * tails + tail

    def pairs(k):
        return [(i, i ^ k ^ parity(k >> 1)) for i in range(blocks)]

    vmem = pl.BlockSpec(memory_space=pltpu.VMEM)
    hbm = pl.BlockSpec(memory_space=pltpu.HBM)
    means_row = means[None, :]
    scales_row = scales[None, :]
    width = -(-causal_count // LANES) * LANES

    held, send, keep, tail = pl.pallas_call(
        lambda *refs: evolve_kernel(blocks, share, FLIGHT, relative_of, *refs),
        out_shape=(
            jax.ShapeDtypeStruct((blocks, share, variants), SMALL),
            jax.ShapeDtypeStruct((half, pheno, share), jnp.bfloat16),
            jax.ShapeDtypeStruct((half, pheno, share), jnp.float32),
            jax.ShapeDtypeStruct((tails, pheno, share), jnp.float32),
        ),
        in_specs=[hbm] * 7,
        out_specs=[vmem] * 4,
        scratch_shapes=[
            pltpu.VMEM((blocks, share, variants), genotypes.dtype),
            pltpu.VMEM((pheno, causal_count), jnp.int32),
            pltpu.VMEM((pheno, causal_count), jnp.float32),
            pltpu.VMEM((1, variants), jnp.float32),
            pltpu.VMEM((1, variants), jnp.float32),
            pltpu.VMEM((1, pheno), jnp.float32),
            pltpu.VMEM((pheno, width), jnp.int32),
            pltpu.VMEM((pheno, width), jnp.int32),
            pltpu.VMEM((pheno, width), jnp.float32),
            pltpu.VMEM((pheno, variants // LANES, LANES), jnp.float32),
            pltpu.VMEM((pheno, variants), jnp.float32),
            pltpu.VMEM((tails, pheno, share), jnp.bfloat16),
            pltpu.SemaphoreType.DMA((blocks,)),
            pltpu.SemaphoreType.DMA((tails,)),
            pltpu.SemaphoreType.DMA((5,)),
        ],
        compiler_params=pltpu.CompilerParams(vmem_limit_bytes=24 * MIB),
        name="evolve",
    )(
        *(
            pltpu.with_memory_space_constraint(x, pltpu.HBM)
            for x in (
                genotypes,
                noise,
                means_row,
                scales_row,
                causal,
                effects,
                heritability[None, :],
            )
        )
    )

    got = lax.ppermute(send, "var", pairs(1))
    chip = [
        keep[i * tails : (i + 1) * tails] + got[i * tails : (i + 1) * tails].astype(jnp.float32)
        for i in range(4)
    ]
    arrived = [
        lax.ppermute(chip[g - 1].astype(jnp.bfloat16), "var", pairs(2 * g)) for g in (1, 2, 3)
    ]
    total = chip[3]
    for other in arrived:
        total = total + other.astype(jnp.float32)

    step = 1
    while step < tails:
        mine = total.astype(jnp.bfloat16)
        other = lax.ppermute(mine, "var", pairs(8 * step))
        other = jnp.concatenate([other[t ^ step][None] for t in range(tails)], axis=0)
        total = mine.astype(jnp.float32) + other.astype(jnp.float32)
        step *= 2

    own = (total + tail).astype(jnp.bfloat16)
    groups = {0: own}
    for g in (1, 2, 3):
        groups[g] = lax.ppermute(own, "var", pairs(2 * g))
    others = {g: lax.ppermute(groups[g], "var", pairs(1)) for g in range(4)}
    first = [(0, g, groups[g]) for g in range(4)] + [(1, g, others[g]) for g in (0, 3, 2)]
    last = [(1, 1, others[1])]

    def places(chosen):
        return [position(core, g, t) for core, g, _ in chosen for t in range(tails)]

    def arrays(chosen):
        return [array for _, _, array in chosen]

    alone = samp == 1
    total_samples = jnp.float32(samples * samp)
    scale_back = float(samples * samp) ** 0.5 if alone else None
    params = pltpu.CompilerParams(vmem_limit_bytes=8 * MIB)
    early, early_column = pl.pallas_call(
        lambda *refs: early_kernel(places(first), *refs),
        out_shape=(
            jax.ShapeDtypeStruct((pheno, variants), jnp.float32),
            jax.ShapeDtypeStruct((pheno, LANES), jnp.float32),
        ),
        in_specs=[vmem] * (1 + len(first)),
        out_specs=[vmem] * 2,
        compiler_params=params,
        name="scan_early",
    )(held, *arrays(first))
    phen_out, scores = pl.pallas_call(
        lambda *refs: late_kernel(
            places(last), scale_back, lambda me: parity(me >> 1), *refs
        ),
        out_shape=(
            jax.ShapeDtypeStruct((pheno, share), jnp.bfloat16),
            jax.ShapeDtypeStruct((pheno, variants), jnp.float32),
        ),
        in_specs=[vmem] * (7 + len(last)),
        out_specs=[vmem] * 2,
        compiler_params=params,
        name="scan_late",
    )(held, means_row, scales_row, own, others[0], early, early_column, *arrays(last))
    if alone:
        return phen_out, scores

    pieces = arrays(first + last)
    column = sum(jnp.sum(piece.astype(jnp.float32), axis=(0, 2)) for piece in pieces)
    score_width = variants // samp
    score_start = lax.axis_index("samp") * score_width
    means_part = lax.dynamic_slice_in_dim(means, score_start, score_width, 0)
    scales_part = lax.dynamic_slice_in_dim(scales, score_start, score_width, 0)
    column_sum = lax.psum(column, "samp")
    correction = column_sum[:, None] * means_part[None, :]
    summed = lax.psum_scatter(scores, "samp", scatter_dimension=1, tiled=True)
    scores = (summed - correction) / (scales_part[None, :] * jnp.sqrt(total_samples))
    return phen_out, scores


def solution(mesh):
    in_specs = (
        P("samp", "var"),
        P("var"),
        P("var"),
        P("rep", None),
        P("rep", None),
        P("rep"),
        P("rep", "samp"),
    )
    out_specs = (P("rep", ("samp", "var")), P("rep", ("var", "samp")))
    return jax.shard_map(
        on_device, mesh=mesh, in_specs=in_specs, out_specs=out_specs, check_vma=False
    )
```

```python
import jax
import jax.numpy as jnp
from jax import lax
from jax.experimental import pallas as pl
from jax.experimental.pallas import tpu as pltpu
from jax.sharding import PartitionSpec as P

LANES = 128
MIB = 1 << 20
SMALL = jnp.float8_e4m3fn
LARGEST = 448.0
EARLY = 2
FLIGHT = 3
CROSS = 1
SHIFT = 16.0
EFFECT_SCALE = 1024.0


def row_scale(values):
    largest = jnp.max(jnp.abs(values), axis=1, keepdims=True)
    scale = jnp.full_like(largest, 2.0**-30)
    for step in (32, 16, 8, 4, 2, 1):
        raised = scale * 2.0**step
        scale = jnp.where(largest * raised <= LARGEST, raised, scale)
    return scale


def split(values, count):
    parts = []
    for i in range(count):
        part = values.astype(SMALL)
        parts.append(part)
        if i + 1 < count:
            values = (values - part.astype(jnp.float32)) * SHIFT
    return jnp.concatenate(parts, axis=0)


def join(sums, count):
    rows = sums.shape[0] // count
    total = sums[(count - 1) * rows :]
    for i in reversed(range(count - 1)):
        total = sums[i * rows : (i + 1) * rows] + total * (1.0 / SHIFT)
    return total


def evolve_kernel(
    blocks,
    share,
    flight,
    relative_of,
    genotypes_hbm,
    noise_hbm,
    means_hbm,
    scales_hbm,
    causal_hbm,
    effects_hbm,
    heritability_hbm,
    held_ref,
    send_ref,
    keep_ref,
    tail_ref,
    staged_ref,
    causal_ref,
    effects_ref,
    means_ref,
    scales_ref,
    heritability_ref,
    high_ref,
    low_ref,
    value_ref,
    beta_ref,
    weight_ref,
    noise_ref,
    block_sem,
    noise_sem,
    small_sem,
):
    pheno, variants = weight_ref.shape
    me = lax.axis_index("var")
    tails = tail_ref.shape[0]
    half = blocks // 2

    def fetch(i):
        start = pl.multiple_of((me ^ relative_of(i, me)) * share, share)
        return pltpu.make_async_copy(
            genotypes_hbm.at[pl.ds(start, share), :], staged_ref.at[i], block_sem.at[i]
        )

    def fetch_noise(t):
        start = pl.multiple_of((me ^ relative_of(blocks - tails + t, me)) * share, share)
        return pltpu.make_async_copy(
            noise_hbm.at[:, pl.ds(start, share)], noise_ref.at[t], noise_sem.at[t]
        )

    small = [
        pltpu.make_async_copy(source, target, small_sem.at[i])
        for i, (source, target) in enumerate(
            (
                (causal_hbm, causal_ref),
                (effects_hbm, effects_ref),
                (scales_hbm, scales_ref),
                (means_hbm, means_ref),
                (heritability_hbm, heritability_ref),
            )
        )
    ]
    for copy in small[:2]:
        copy.start()
    for i in range(EARLY):
        fetch(i).start()
    for copy in small[2:]:
        copy.start()
    for t in range(tails):
        fetch_noise(t).start()

    causal_count = causal_ref.shape[1]
    high_count = variants // LANES
    high_ref[...] = jnp.full(high_ref.shape, -1, jnp.int32)
    low_ref[...] = jnp.zeros(low_ref.shape, jnp.int32)
    value_ref[...] = jnp.zeros(value_ref.shape, jnp.float32)
    for copy in small[:2]:
        copy.wait()
    for i in range(EARLY, flight):
        fetch(i).start()
    local = causal_ref[...] - me * variants
    inside = (local >= 0) & (local < variants)
    high_ref[:, :causal_count] = jnp.where(inside, local // LANES, -1)
    low_ref[:, :causal_count] = jnp.where(inside, local % LANES, 0)
    value_ref[:, :causal_count] = effects_ref[...] * EFFECT_SCALE
    width = high_ref.shape[1]
    high_iota = lax.broadcasted_iota(jnp.int32, (high_count, width), 0)
    low_iota = lax.broadcasted_iota(jnp.int32, (LANES, width), 0).astype(jnp.int16)

    def build(p):
        row = pl.ds(p, 1)
        value = jnp.where(high_ref[row, :] == high_iota, value_ref[row, :], 0.0)
        low = jnp.broadcast_to(low_ref[row, :], (LANES, width)).astype(jnp.int16)
        hits = jnp.where(low == low_iota, jnp.bfloat16(1), jnp.bfloat16(0)).astype(SMALL)
        sums = lax.dot_general(
            split(value, 4), hits, (((1,), (1,)), ((), ())), preferred_element_type=jnp.float32
        )
        beta_ref[p] = join(sums, 4) * (1.0 / EFFECT_SCALE)

    steps = half
    per_step = -(-pheno // steps)

    def build_step(i, carry):
        @pl.when(flight + i < blocks)
        def _():
            fetch(flight + i).start()

        for j in range(per_step):
            build(jnp.minimum(i * per_step + j, pheno - 1))
        return carry

    lax.fori_loop(0, steps, build_step, 0, unroll=True)
    for i in range(flight + steps, blocks):
        fetch(i).start()

    for copy in small[2:]:
        copy.wait()
    offset = jnp.zeros((pheno, LANES), jnp.float32)
    for h in range(high_count):
        lanes = slice(h * LANES, (h + 1) * LANES)
        weight = (beta_ref[:, h, :] / scales_ref[:, lanes]).astype(jnp.bfloat16)
        weight = weight.astype(jnp.float32)
        weight_ref[:, lanes] = weight
        offset += weight * means_ref[:, lanes]
    offset = jnp.sum(offset, axis=1, keepdims=True)

    square = (pheno, pheno)
    diagonal = lax.broadcasted_iota(jnp.int32, square, 0) == lax.broadcasted_iota(
        jnp.int32, square, 1
    )
    share_genetic = jnp.sum(
        jnp.where(diagonal, jnp.broadcast_to(heritability_ref[...], square), 0.0),
        axis=1,
        keepdims=True,
    )
    heavy = jnp.sqrt(share_genetic)
    light = jnp.sqrt(1.0 - share_genetic)
    scale = row_scale(weight_ref[...])
    weights = split(weight_ref[...] * scale, 2)
    factor = heavy / scale
    shift = heavy * offset

    for start in range(0, blocks, 2):
        for i in (start, start + 1):
            fetch(i).wait()
        for i in (start, start + 1):
            block = staged_ref[i].astype(SMALL)
            held_ref[i] = block
            sums = lax.dot_general(
                weights, block, (((1,), (1,)), ((), ())), preferred_element_type=jnp.float32
            )
            value = join(sums, 2) * factor - shift
            if i < half:
                send_ref[i] = value.astype(send_ref.dtype)
            else:
                keep_ref[i - half] = value.astype(keep_ref.dtype)
    for t in range(tails):
        fetch_noise(t).wait()
        tail_ref[t] = light * noise_ref[t].astype(jnp.float32)


def scan_pieces(order, held_ref, pieces):
    values = [piece[j].astype(jnp.float32) for piece in pieces for j in range(piece.shape[0])]
    largest = jnp.abs(values[0])
    column = values[0]
    for value in values[1:]:
        largest = jnp.maximum(largest, jnp.abs(value))
        column = column + value
    scale = row_scale(largest)
    total = None
    for i, value in enumerate(values):
        part = jnp.dot(
            split(value * scale, 2), held_ref[order[i]], preferred_element_type=jnp.float32
        )
        total = part if total is None else total + part
    return join(total, 2) / scale, jnp.sum(column, axis=1, keepdims=True)


def early_kernel(order, held_ref, *refs):
    pieces = refs[:-2]
    total_ref, column_ref = refs[-2:]
    total, column = scan_pieces(order, held_ref, pieces)
    total_ref[...] = total
    column_ref[...] = jnp.broadcast_to(column, column_ref.shape)


def late_kernel(
    order, scale_back, swapped, held_ref, means_ref, scales_ref, own_ref, other_ref, *refs
):
    early_ref, early_column_ref = refs[:2]
    pieces = refs[2:-2]
    phen_ref, out_ref = refs[-2:]
    mine = swapped(lax.axis_index("var")) == 0
    phen_ref[...] = jnp.where(mine, own_ref[0], other_ref[0])
    total, column = scan_pieces(order, held_ref, pieces)
    total = total + early_ref[...]
    column = column + early_column_ref[:, :1]
    if scale_back is None:
        out_ref[...] = total
    else:
        out_ref[...] = (total - column * means_ref[...]) / (scales_ref[...] * scale_back)


def on_device(genotypes, means, scales, causal, effects, heritability, noise):
    samples, variants = genotypes.shape
    pheno, causal_count = causal.shape
    blocks = lax.axis_size("var")
    samp = lax.axis_size("samp")
    share = samples // blocks
    bits = blocks.bit_length() - 1
    if blocks != 1 << bits or bits < 3:
        raise ValueError("var size")
    tails = blocks // 8

    half = blocks // 2

    def parity(chip):
        total = 0
        for bit in range(bits - 1):
            if CROSS >> bit & 1:
                total = total ^ (chip >> bit & 1)
        return total

    def relative_of(i, me):
        core = 1 - i // half
        group = (i % half // tails + 1) % 4
        return (core ^ parity(me >> 1)) + 2 * group + 8 * (i % tails)

    def position(core, group, tail):
        return (1 - core) * half + (group + 3) % 4 * tails + tail

    def pairs(k):
        return [(i, i ^ k ^ parity(k >> 1)) for i in range(blocks)]

    vmem = pl.BlockSpec(memory_space=pltpu.VMEM)
    hbm = pl.BlockSpec(memory_space=pltpu.HBM)
    means_row = means[None, :]
    scales_row = scales[None, :]
    width = -(-causal_count // LANES) * LANES

    held, send, keep, tail = pl.pallas_call(
        lambda *refs: evolve_kernel(blocks, share, FLIGHT, relative_of, *refs),
        out_shape=(
            jax.ShapeDtypeStruct((blocks, share, variants), SMALL),
            jax.ShapeDtypeStruct((half, pheno, share), jnp.bfloat16),
            jax.ShapeDtypeStruct((half, pheno, share), jnp.float32),
            jax.ShapeDtypeStruct((tails, pheno, share), jnp.float32),
        ),
        in_specs=[hbm] * 7,
        out_specs=[vmem] * 4,
        scratch_shapes=[
            pltpu.VMEM((blocks, share, variants), genotypes.dtype),
            pltpu.VMEM((pheno, causal_count), jnp.int32),
            pltpu.VMEM((pheno, causal_count), jnp.float32),
            pltpu.VMEM((1, variants), jnp.float32),
            pltpu.VMEM((1, variants), jnp.float32),
            pltpu.VMEM((1, pheno), jnp.float32),
            pltpu.VMEM((pheno, width), jnp.int32),
            pltpu.VMEM((pheno, width), jnp.int32),
            pltpu.VMEM((pheno, width), jnp.float32),
            pltpu.VMEM((pheno, variants // LANES, LANES), jnp.float32),
            pltpu.VMEM((pheno, variants), jnp.float32),
            pltpu.VMEM((tails, pheno, share), jnp.bfloat16),
            pltpu.SemaphoreType.DMA((blocks,)),
            pltpu.SemaphoreType.DMA((tails,)),
            pltpu.SemaphoreType.DMA((5,)),
        ],
        compiler_params=pltpu.CompilerParams(vmem_limit_bytes=24 * MIB),
        name="evolve",
    )(
        *(
            pltpu.with_memory_space_constraint(x, pltpu.HBM)
            for x in (
                genotypes,
                noise,
                means_row,
                scales_row,
                causal,
                effects,
                heritability[None, :],
            )
        )
    )

    got = lax.ppermute(send, "var", pairs(1))
    chip = [
        keep[i * tails : (i + 1) * tails] + got[i * tails : (i + 1) * tails].astype(jnp.float32)
        for i in range(4)
    ]
    arrived = [
        lax.ppermute(chip[g - 1].astype(jnp.bfloat16), "var", pairs(2 * g)) for g in (1, 2, 3)
    ]
    total = chip[3]
    for other in arrived:
        total = total + other.astype(jnp.float32)

    step = 1
    while step < tails:
        mine = total.astype(jnp.bfloat16)
        other = lax.ppermute(mine, "var", pairs(8 * step))
        other = jnp.concatenate([other[t ^ step][None] for t in range(tails)], axis=0)
        total = mine.astype(jnp.float32) + other.astype(jnp.float32)
        step *= 2

    own = (total + tail).astype(jnp.bfloat16)
    groups = {0: own}
    for g in (1, 2, 3):
        groups[g] = lax.ppermute(own, "var", pairs(2 * g))
    others = {g: lax.ppermute(groups[g], "var", pairs(1)) for g in range(4)}
    first = [(0, g, groups[g]) for g in (0, 2, 3)] + [(1, g, others[g]) for g in (0, 3)]
    last = [(0, 1, groups[1]), (1, 1, others[1]), (1, 2, others[2])]

    def places(chosen):
        return [position(core, g, t) for core, g, _ in chosen for t in range(tails)]

    def arrays(chosen):
        return [array for _, _, array in chosen]

    alone = samp == 1
    total_samples = jnp.float32(samples * samp)
    scale_back = float(samples * samp) ** 0.5 if alone else None
    params = pltpu.CompilerParams(vmem_limit_bytes=8 * MIB)
    early, early_column = pl.pallas_call(
        lambda *refs: early_kernel(places(first), *refs),
        out_shape=(
            jax.ShapeDtypeStruct((pheno, variants), jnp.float32),
            jax.ShapeDtypeStruct((pheno, LANES), jnp.float32),
        ),
        in_specs=[vmem] * (1 + len(first)),
        out_specs=[vmem] * 2,
        compiler_params=params,
        name="scan_early",
    )(held, *arrays(first))
    phen_out, scores = pl.pallas_call(
        lambda *refs: late_kernel(
            places(last), scale_back, lambda me: parity(me >> 1), *refs
        ),
        out_shape=(
            jax.ShapeDtypeStruct((pheno, share), jnp.bfloat16),
            jax.ShapeDtypeStruct((pheno, variants), jnp.float32),
        ),
        in_specs=[vmem] * (7 + len(last)),
        out_specs=[vmem] * 2,
        compiler_params=params,
        name="scan_late",
    )(held, means_row, scales_row, own, others[0], early, early_column, *arrays(last))
    if alone:
        return phen_out, scores

    pieces = arrays(first + last)
    column = sum(jnp.sum(piece.astype(jnp.float32), axis=(0, 2)) for piece in pieces)
    score_width = variants // samp
    score_start = lax.axis_index("samp") * score_width
    means_part = lax.dynamic_slice_in_dim(means, score_start, score_width, 0)
    scales_part = lax.dynamic_slice_in_dim(scales, score_start, score_width, 0)
    column_sum = lax.psum(column, "samp")
    correction = column_sum[:, None] * means_part[None, :]
    summed = lax.psum_scatter(scores, "samp", scatter_dimension=1, tiled=True)
    scores = (summed - correction) / (scales_part[None, :] * jnp.sqrt(total_samples))
    return phen_out, scores


def solution(mesh):
    in_specs = (
        P("samp", "var"),
        P("var"),
        P("var"),
        P("rep", None),
        P("rep", None),
        P("rep"),
        P("rep", "samp"),
    )
    out_specs = (P("rep", ("samp", "var")), P("rep", ("var", "samp")))
    return jax.shard_map(
        on_device, mesh=mesh, in_specs=in_specs, out_specs=out_specs, check_vma=False
    )
```
